512 devices in a mesh: batch: 16 (over z_hi, x), tm: 32 (over y, z_lo, core).
Axes of the slice: x: 4, y: 4, z: 16 (z_hi: 4, z_lo: 4; z = z_hi * 4 + z_lo), core: 2. Of those that a mesh axis runs over, the one named last changes fastest.
Arguments:
- raw: bfloat16 [16, 4096, 640], P('batch', 'tm'), may hold values from -6 to 6
- w_conv: bfloat16 [1280, 512], replicated, may hold values from -0.15625 to 0.15625
- w_query: bfloat16 [512, 1024], replicated, may hold values from -0.25 to 0.25
- w_key: bfloat16 [512, 1024], replicated, may hold values from -0.25 to 0.25
- w_pred: bfloat16 [2, 512, 512], replicated, may hold values from -0.25 to 0.25
- log_decay: float32 [16, 8, 4096], P('batch', None, 'tm'), may hold values from -1 to 0
- lengths: int32 [16], P('batch'), may hold values from 2048 to 4096, as said below
- neg_offset: int32 [16, 4096, 3], P('batch', 'tm'), may hold values from 0 to 14, all different within a row; in each aligned block of 128 rows (0 to 127, 128 to 255, ..., all dimensions but the last counted through in order) at most 39 rows name the same one
- neg_frame: int32 [16, 4096, 3], P('batch', 'tm'), may hold values from 0 to 127
Outputs:
- logits: float32 [16, 2, 4, 4096], P('batch', None, None, 'tm')
The draws below stay inside these ranges and needn't reach their ends.
Inputs may be any that keep to these rules, and one draw needn't show every extreme that they name: `neg_offset`: in each device's 128 frames (an aligned block of rows), a frame's 3 offsets are distinct, and no offset is named by more than 39 of those frames; some offset is named by exactly 39 of them. `neg_frame`: a frame of the anchor's own time shard of 128 frames. `lengths`: one stream holds all 4096 frames and another exactly half of them.
All inputs are finite; a program needn't handle non-finite values.
Results may differ from the reference program's by a relative error of at most 0.0094.
Values may be sent and summed in bfloat16 or wider, within the bound.
A program may use at most 64 MiB of HBM per device.

```python
import math
import jax
import jax.numpy as jnp
import numpy as np
from jax import lax

E = 512
DA = 1024
H = 8
K = 2
NNEG = 3
SPAN = 128
FD = 128
FRAME_W = 640
GROUPS = 16
TF = 4096
CAP = 39


def draw_log_decay(key, part):
    keys = jax.random.split(key, 7)
    slow_share = 0.5
    slow = jax.random.uniform(keys[0], (GROUPS, H, 1)) < slow_share
    slow_rate = jnp.exp(jax.random.uniform(keys[1], (GROUPS, H, 1), minval=jnp.log(0.05), maxval=0.0)) / TF
    fast_rate = jax.random.uniform(keys[2], (GROUPS, H, 1), minval=1.0 / 50.0, maxval=1.0 / 30.0)
    starting_shift_amount = jnp.where(slow, slow_rate, fast_rate)
    shard_count = TF // FD
    partition_factor = jnp.exp(jax.random.uniform(keys[3], (GROUPS, H, shard_count), minval=jnp.log(0.5), maxval=jnp.log(2.0)))
    partition_factor = jnp.repeat(partition_factor, FD, axis=2)
    rough_guess_value = jax.random.uniform(keys[4], (GROUPS, H, TF), minval=0.5, maxval=1.5)
    drawn_location_array = jax.random.randint(keys[5], (GROUPS, H, 2), 0, TF)
    timestep_ordinal_array = jnp.arange(TF, dtype=jnp.int32)
    run_count_span = jnp.any(timestep_ordinal_array[None, None, :, None] == drawn_location_array[:, :, None, :], axis=-1)
    noise_discrimination_objective = jax.random.uniform(keys[6], (GROUPS, H, TF), minval=0.2, maxval=0.4)
    drawn_ordinal = -(starting_shift_amount * partition_factor * rough_guess_value) + jnp.where(run_count_span, jnp.log1p(-noise_discrimination_objective), 0.0)
    return drawn_ordinal.astype(jnp.float32)


def draw_lengths(key, part):
    keys = jax.random.split(key, 3)
    drawn_ordinal = jax.random.randint(keys[0], (GROUPS,), TF // 2, TF + 1)
    full_index = jax.random.randint(keys[1], (), 0, GROUPS)
    half_index = (full_index + 1 + jax.random.randint(keys[2], (), 0, GROUPS - 1)) % GROUPS
    return drawn_ordinal.at[full_index].set(TF).at[half_index].set(TF // 2).astype(jnp.int32)


def plant(result, key, least, high):
    shape = result.shape
    spot = [jax.random.randint(jax.random.fold_in(key, axis), (), 0, shape[axis]) for axis in range(len(shape))]
    result = result.at[tuple(spot)].set(least)
    longest = shape.index(max(shape))
    spot[longest] = (spot[longest] + 1) % shape[longest]
    return result.at[tuple(spot)].set(high)


def level_of(key, shape, pieces, least, largest):
    gain, own = 1.0, jax.random.fold_in(key, 6)
    for axis_at, shards_of in pieces:
        draws = jnp.exp(jax.random.uniform(jax.random.fold_in(own, axis_at), (shards_of,), jnp.float32, least / len(pieces), largest / len(pieces)))
        gain = gain * jnp.repeat(draws, shape[axis_at] // shards_of).reshape([-1 if axis == axis_at else 1 for axis in range(len(shape))])
    return gain


def routed_block(rng, own, number, rows, amount, top, limit, lean):
    order = jax.random.permutation(rng, amount)
    crowded, usual = portions_of(amount, rows * top, limit, lean, True), portions_of(amount, rows * top, limit, lean, False)
    places = jnp.arange(amount)

    def named(tallies, offset_by):
        used = int((tallies > 0).sum())
        fixed = max(1, used // 4)
        passed = fixed + (places - fixed + offset_by * (used - fixed)) % max(1, amount - fixed)
        return jnp.zeros((amount,), jnp.int32).at[order[jnp.where(places < fixed, places, passed)]].set(jnp.asarray(tallies, jnp.int32))

    tallies = jnp.where(number % 4 == 0, named(crowded, number // 4), named(usual, number - number // 4 - 1))
    mixed = jax.random.permutation(jax.random.fold_in(own, 3), amount)
    source_of, sink = mixed[0:amount // 2 * 2:2], mixed[1:amount // 2 * 2:2]
    margin = jnp.minimum(tallies[source_of] - 1, limit - tallies[sink]) // 2
    margin = jnp.where((source_of == order[0]) | (sink == order[0]) | (tallies[sink] == 0), 0, jnp.maximum(margin, 0))
    passed = jax.random.randint(jax.random.fold_in(own, 4), (amount // 2,), 0, 1 << 20) % (margin + 1)
    tallies = tallies.at[source_of].add(-passed).at[sink].add(passed)
    labels = jnp.searchsorted(jnp.cumsum(tallies), jnp.arange(rows * top), side="right").astype(jnp.int32)
    table = labels.reshape(top, rows).T
    table = table[jax.random.permutation(jax.random.fold_in(own, 1), rows)]
    offset_by = jax.random.randint(jax.random.fold_in(own, 2), (rows, 1), 0, top)
    return jnp.take_along_axis(table, (jnp.arange(top)[None, :] + offset_by) % top, axis=1)


def portions_of(count, total, most, lean, full):
    portions = [(1 << 20) // math.isqrt(rank ** lean) + 1 for rank in range(1, count + 1)]
    largest = most if full else min(most, max(-(-total // count), total * portions[0] // sum(portions)))
    least = 1 if total - largest >= count - 1 else 0
    holding, surplus = [largest] + [least] * (count - 1), total - largest - least * (count - 1)
    while surplus > 0:
        free = [i for i in range(1, count) if holding[i] < largest] or [i for i in range(1, count) if holding[i] < most]
        pool, budget = sum([portions[i] for i in free]), surplus
        for i in free:
            more = min(most - holding[i], max(1, budget * portions[i] // pool), surplus)
            holding[i] = holding[i] + more
            surplus = surplus - more
    return np.array(holding)


def bell_draw(rng, shape, spread, most, shards=(), held_as=jnp.bfloat16):
    values = jax.random.normal(rng, shape, jnp.float32) * spread
    if len(shards) > 0:
        values = level_of(rng, shape, shards, -0.22, 0.18) * values
    return jnp.clip(values, min=-most, max=most).astype(held_as)


def setup_inputs(seed: int = 0) -> dict:
    splits = jax.random.split(jax.random.key(seed), 10)
    raw = bell_draw(splits[0], (GROUPS, TF, FRAME_W), 1.0, 6.0, ((0, 16), (1, 32)))
    w_conv = bell_draw(splits[1], (2 * FRAME_W, E), (2 * FRAME_W) ** -0.5, 0.15625)
    w_query = bell_draw(splits[2], (E, DA), E ** -0.5, 0.25)
    w_key = bell_draw(splits[3], (E, DA), E ** -0.5, 0.25)
    w_pred = bell_draw(splits[4], (K, E, E), E ** -0.5, 0.25)
    log_decay = draw_log_decay(jax.random.fold_in(splits[9], 71), 0)
    lengths = draw_lengths(jax.random.fold_in(splits[9], 71), 0)
    neg_offset_keys = jax.random.split(jax.random.fold_in(splits[7], 1), GROUPS * TF // FD)
    neg_offset_turns = jax.random.permutation(jax.random.fold_in(splits[7], 3), GROUPS * TF // FD)
    neg_offset = jax.vmap(lambda own, number: routed_block(jax.random.fold_in(splits[7], 2), own, number, FD, GROUPS - 1, NNEG, CAP, 2))(neg_offset_keys, neg_offset_turns).reshape((GROUPS, TF, NNEG))
    neg_frame = plant(jax.random.randint(splits[8], (GROUPS, TF, NNEG), 0, FD), jax.random.fold_in(splits[8], 1), 0, FD - 1).astype(jnp.int32)
    return {"raw": raw, "w_conv": w_conv, "w_query": w_query, "w_key": w_key, "w_pred": w_pred, "log_decay": log_decay, "lengths": lengths, "neg_offset": neg_offset, "neg_frame": neg_frame}


def rms_rows(values):
    return values * lax.rsqrt(lax.optimization_barrier(jnp.mean(values * values, axis=-1, keepdims=True)) + 1e-05)

def round_half(values):
    return lax.optimization_barrier(values.astype(jnp.bfloat16)).astype(jnp.float32)

def reference(raw, w_conv, w_query, w_key, w_pred, log_decay, lengths, neg_offset, neg_frame):
    head_key = DA // H
    head_value = E // H
    n_blocks = TF // SPAN
    timestep_ordinal_array = jnp.arange(TF, dtype=jnp.int32)
    valid_mask = (timestep_ordinal_array[None, :] < lengths[:, None]).astype(jnp.float32)
    earlier = jnp.concatenate([jnp.zeros((GROUPS, 1, FRAME_W), raw.dtype), raw[:, :-1]], axis=1)
    hidden = jnp.dot(earlier.reshape(GROUPS * TF, FRAME_W), w_conv[:FRAME_W], preferred_element_type=jnp.float32)
    hidden = hidden + jnp.dot(raw.reshape(GROUPS * TF, FRAME_W), w_conv[FRAME_W:], preferred_element_type=jnp.float32)
    normed = rms_rows(jax.nn.gelu(hidden)).reshape(GROUPS, TF, E) * valid_mask[:, :, None]
    encoded = normed.astype(jnp.bfloat16)
    flat_enc = encoded.reshape(GROUPS * TF, E)
    queries = jnp.dot(flat_enc, w_query, preferred_element_type=jnp.float32).astype(jnp.bfloat16)
    key_rows = jnp.dot(flat_enc, w_key, preferred_element_type=jnp.float32).astype(jnp.bfloat16)
    queries = queries.reshape(GROUPS, n_blocks, SPAN, H, head_key)
    key_rows = key_rows.reshape(GROUPS, n_blocks, SPAN, H, head_key)
    values = encoded.reshape(GROUPS, n_blocks, SPAN, H, head_value)
    decay_rates = log_decay.reshape(GROUPS, H, n_blocks, SPAN)
    scale = 1.0 / math.sqrt(head_key)
    causal = jnp.arange(SPAN)[:, None] >= jnp.arange(SPAN)[None, :]

    def block_step(running, inputs):
        query_blk, key_blk, value_blk, rate_blk = inputs
        query_f = query_blk.astype(jnp.float32)
        key_f = key_blk.astype(jnp.float32)
        value_f = value_blk.astype(jnp.float32)
        log_cum = jnp.cumsum(rate_blk, axis=-1)
        scores = jnp.einsum('gthd,gshd->ghts', query_f, key_f)
        log_gap = log_cum[:, :, :, None] - log_cum[:, :, None, :]
        weight = jnp.where(causal, jnp.exp(jnp.minimum(log_gap, 0.0)), 0.0)
        weights_bf = round_half(scores * weight * scale)
        inside = jnp.einsum('ghts,gshe->gthe', weights_bf, value_f)
        entry_bf = round_half(running)
        carried = jnp.einsum('gthd,ghde->gthe', query_f, entry_bf)
        carried = carried * jnp.transpose(jnp.exp(log_cum) * scale, (0, 2, 1))[..., None]
        to_end = jnp.exp(log_cum[:, :, -1:] - log_cum)
        weighted = round_half(key_f * jnp.transpose(to_end, (0, 2, 1))[..., None])
        updated = jnp.exp(log_cum[:, :, -1])[:, :, None, None] * running
        updated = updated + jnp.einsum('gshd,gshe->ghde', weighted, value_f)
        return (updated, inside + carried)
    inputs = (jnp.moveaxis(queries, 1, 0), jnp.moveaxis(key_rows, 1, 0), jnp.moveaxis(values, 1, 0), jnp.moveaxis(decay_rates, 2, 0))
    start = jnp.zeros((GROUPS, H, head_key, head_value), jnp.float32)
    _, attended = lax.scan(block_step, start, inputs)
    attended = jnp.moveaxis(attended, 0, 1).reshape(GROUPS, TF, H, head_value)
    context = rms_rows(attended).reshape(GROUPS * TF, E).astype(jnp.bfloat16)
    inv_width = 1.0 / math.sqrt(E)
    shard_start = timestep_ordinal_array // FD * FD
    group_ids = jnp.arange(GROUPS, dtype=jnp.int32)
    step_rows = []
    for ahead_step in range(K):
        predicted = jnp.dot(context, w_pred[ahead_step], preferred_element_type=jnp.float32).astype(jnp.bfloat16)
        predicted = predicted.reshape(GROUPS, TF, E)
        targets = jnp.concatenate([encoded[:, ahead_step + 1:], jnp.zeros((GROUPS, ahead_step + 1, E), jnp.bfloat16)], axis=1)
        positive = jnp.einsum('gte,gte->gt', predicted.astype(jnp.float32), targets.astype(jnp.float32)) * inv_width

        def score_group(item):
            group_id, offsets, frames_in, pred_rows = item
            target_group = (group_id + offsets + 1) % GROUPS
            target_frame = shard_start[:, None] + frames_in
            picked = encoded[target_group, target_frame]
            return jnp.einsum('te,tje->jt', pred_rows.astype(jnp.float32), picked.astype(jnp.float32)) * inv_width
        negative = lax.map(score_group, (group_ids, neg_offset, neg_frame, predicted))
        step_rows.append(jnp.concatenate([positive[:, None, :], negative], axis=1))
    logits = jnp.stack(step_rows, axis=1)
    return logits * valid_mask[:, None, None, :]
```

```python
import functools
import math

import jax
import jax.numpy as jnp
from jax import lax
from jax.experimental import pallas as pl
from jax.experimental.pallas import tpu as pltpu
from jax.sharding import PartitionSpec as P

MESH = pl.DeviceIdType.MESH
F32, BF16, I32 = jnp.float32, jnp.bfloat16, jnp.int32
FD, E, DA, H, FRAME_W, K, NNEG = 128, 512, 1024, 8, 640, 2, 3
DK, DV = DA // H, E // H
SLOT = 48
HALF = FD // 2
MSG = DV + 16
YMSG = DV + 8


def nt(a, b):
    return lax.dot_general(a, b, (((1,), (1,)), ((), ())), preferred_element_type=F32)


def nn(a, b):
    return jnp.dot(a, b, preferred_element_type=F32)


def iota(shape, axis):
    return lax.broadcasted_iota(I32, shape, axis)


def kernel(
    raw_hbm, wc_hbm, wq_hbm, wk_hbm, wp_hbm, ld_hbm, aux_hbm, out_ref,
    raw, wc, wq, wk, wp, ld, aux, halo, fut, want, asked, grid, pick, rows,
    msg_out, msg_in, y_out, y_in, ent_out, ent, q_s, inside,
    load_sem, halo_sem, fut_sem, ask_sem, near_sem, far_sem, row_sem, msg_sem, y_sem, ent_sem,
):
    b, m = lax.axis_index("batch"), lax.axis_index("tm")
    zh, x = b // 4, b % 4
    y, i = m // 8, m % 8

    def at(zz=None, xx=None, tm=None):
        zz = zh if zz is None else zz
        xx = x if xx is None else xx
        return (zz * 4 + xx, m if tm is None else tm)

    def remote(src, dst, sems, index, dev):
        return pltpu.make_async_remote_copy(
            src_ref=src, dst_ref=dst, send_sem=sems.at[(0, *index)], recv_sem=sems.at[(1, *index)],
            device_id=dev, device_id_type=MESH,
        )

    z_up, z_dn = at(zz=(zh + 1) % 4), at(zz=(zh + 3) % 4)
    x_of = [at(xx=(x + d) % 4) for d in range(4)]
    row_of = [at(tm=y * 8 + (i + d) % 8) for d in range(8)]
    y_of = [at(tm=((y + d) % 4) * 8 + i) for d in range(4)]
    nxt, prv = at(tm=jnp.minimum(m + 1, 31)), at(tm=jnp.maximum(m - 1, 0))
    has_next, has_prev = m < 31, m > 0
    edge_next = jnp.logical_and(i == 7, has_next)
    edge_prev = jnp.logical_and(i == 0, has_prev)

    barrier = pltpu.get_barrier_semaphore()
    for dev in [z_up, z_dn] + x_of[1:] + row_of[1:] + y_of[1:]:
        pl.semaphore_signal(barrier, inc=1, device_id=dev, device_id_type=MESH)

    @pl.when(edge_next)
    def _():
        pl.semaphore_signal(barrier, inc=1, device_id=nxt, device_id_type=MESH)

    @pl.when(edge_prev)
    def _():
        pl.semaphore_signal(barrier, inc=1, device_id=prv, device_id_type=MESH)

    loads = [
        pltpu.make_async_copy(src, dst, load_sem.at[n])
        for n, (src, dst) in enumerate(
            [(raw_hbm.at[0], raw), (wc_hbm, wc), (aux_hbm, aux), (ld_hbm.at[0], ld),
             (wk_hbm, wk), (wq_hbm, wq), (wp_hbm, wp)]
        )
    ]
    for load in loads:
        load.start()

    loads[2].wait()
    lane = iota((FD, FD), 1)
    sub = iota((FD, FD), 0)
    rel_j, frame_j = [], []
    for j in range(NNEG):
        group = (b + aux[j : j + 1, :] + 1) & 15
        rel_j.append((((zh - (group >> 2)) & 3) << 2) | ((x - (group & 3)) & 3))
        frame_j.append(aux[3 + j : 4 + j, :])
    rel_rows = iota((16, FD), 0)
    hit = [jnp.where(rel_rows == rel_j[j], 1, 0) for j in range(NNEG)]
    named = hit[0] + hit[1] + hit[2]
    frame_of = hit[0] * frame_j[0] + hit[1] * frame_j[1] + hit[2] * frame_j[2]
    upto = jnp.where(sub <= lane, 1.0, 0.0).astype(BF16)
    rank = nn(named.astype(F32).astype(BF16), upto).astype(I32) - 1
    spot = [jnp.sum(hit[j] * (rel_rows * SLOT + rank), axis=0, keepdims=True) for j in range(NNEG)]
    code = jnp.where(named > 0, rank, -1)
    slot_rows = iota((SLOT, FD), 0)
    slot_lane = iota((SLOT, FD), 1)
    wanted = jnp.zeros((SLOT, FD), I32)
    for r in range(1, 16):
        column = jnp.sum(
            jnp.where(slot_rows == code[r : r + 1, :], frame_of[r : r + 1, :].astype(F32), 0.0), axis=1, keepdims=True
        )
        wanted = jnp.where(slot_lane == r, column.astype(I32), wanted)
    want[...] = wanted

    loads[3].wait()
    cum = ld[...]
    lane8 = iota((H, FD), 1)
    for shift in (1, 2, 4, 8, 16, 32, 64):
        cum = cum + jnp.where(lane8 >= shift, pltpu.roll(cum, shift, 1), 0.0)
    cum_col = jnp.concatenate([cum, jnp.zeros((FD - H, FD), F32)], axis=0).T
    total = jnp.sum(jnp.where(lane8 == FD - 1, cum, 0.0), axis=1, keepdims=True)
    total_row = jnp.broadcast_to(total, (H, FD))

    loads[0].wait()
    loads[1].wait()
    before = nn(raw[...], wc[:FRAME_W, :])
    now = nn(raw[...], wc[FRAME_W:, :])

    pl.semaphore_wait(barrier, 15 + jnp.where(edge_next, 1, 0) + jnp.where(edge_prev, 1, 0))
    halo_copy = remote(raw.at[pl.ds(FD - 16, 16), :], halo, halo_sem, (), nxt)

    @pl.when(has_next)
    def _():
        halo_copy.start()

    asks = [remote(want, asked.at[d], ask_sem, (d,), x_of[(4 - d) % 4]) for d in range(1, 4)]
    for copy in asks:
        copy.start()

    @pl.when(has_prev)
    def _():
        halo_copy.wait_recv()

    @pl.when(jnp.logical_not(has_prev))
    def _():
        halo[...] = jnp.zeros_like(halo)

    edge = nn(halo[...], wc[:FRAME_W, :])
    first = iota((FD, E), 0) == 0
    hidden = now + jnp.where(first, jnp.broadcast_to(edge[15:16, :], (FD, E)), pltpu.roll(before, 1, 0))
    u = jax.nn.gelu(hidden)
    normed = u * lax.rsqrt(jnp.mean(u * u, axis=-1, keepdims=True) + 1e-05)
    length = aux[6:7, :]
    valid_rows = jnp.where(sub + m * FD < length, 1.0, 0.0)
    enc = (normed * jnp.concatenate([valid_rows] * 4, axis=1)).astype(BF16)
    grid[0] = enc

    low, high = pl.ds(0, HALF), pl.ds(HALF, HALF)
    up = [remote(grid.at[0, part, :], grid.at[1, part, :], near_sem, (0, n), z_up) for n, part in enumerate((low, high))]
    dn = [remote(grid.at[0, part, :], grid.at[3, part, :], near_sem, (1, n), z_dn) for n, part in enumerate((high, low))]
    far_up = remote(grid.at[1, low, :], grid.at[2, low, :], far_sem, (0,), z_up)
    far_dn = remote(grid.at[3, high, :], grid.at[2, high, :], far_sem, (1,), z_dn)
    for n in range(2):
        up[n].start()
        dn[n].start()
    fut_copy = remote(grid.at[0, pl.ds(0, 16), :], fut, fut_sem, (), prv)

    @pl.when(has_prev)
    def _():
        fut_copy.start()

    loads[4].wait()
    enc_t = [enc[:, c * FD : (c + 1) * FD].T for c in range(E // FD)]
    value_t = [enc_t[h // 2][(h % 2) * DV : (h % 2 + 1) * DV, :] for h in range(H)]
    keys = nn(enc, wk[...]).astype(BF16)
    lane16 = iota((16, FD), 0)
    for h in range(H):
        key = keys[:, h * DK : (h + 1) * DK]
        to_end = jnp.exp(total_row[h : h + 1, :] - jnp.broadcast_to(cum_col[:, h : h + 1], (FD, FD)))
        weighted = (key.astype(F32) * to_end).astype(BF16)
        state = nn(value_t[h], weighted)
        msg_out[h, pl.ds(0, DV), :] = state.astype(BF16)
        whole = total_row[h : h + 1, :]
        hi = whole.astype(BF16).astype(F32)
        mid = (whole - hi).astype(BF16).astype(F32)
        lo = whole - hi - mid
        pieces = jnp.where(lane16 == 0, hi, jnp.where(lane16 == 1, mid, jnp.where(lane16 == 2, lo, 0.0)))
        msg_out[h, pl.ds(DV, 16), :] = pieces.astype(BF16)
    mine = pltpu.make_async_copy(msg_out.at[i], msg_in.at[i], load_sem.at[7])
    mine.start()
    msgs = [remote(msg_out.at[(i + d) % 8], msg_in.at[i], msg_sem, (d,), row_of[d]) for d in range(1, 8)]
    for copy in msgs:
        copy.start()

    loads[5].wait()
    queries = nn(enc, wq[...]).astype(BF16)
    q_s[...] = queries
    scale = 1.0 / math.sqrt(DK)
    for h in range(H):
        key = keys[:, h * DK : (h + 1) * DK]
        query = queries[:, h * DK : (h + 1) * DK]
        gap = cum[h : h + 1, :] - jnp.broadcast_to(cum_col[:, h : h + 1], (FD, FD))
        weight = jnp.where(sub <= lane, jnp.exp(jnp.minimum(gap, 0.0)), 0.0)
        probs_t = (nt(key, query) * weight * scale).astype(BF16)
        inside[h] = nn(value_t[h], probs_t)

    for copy in asks:
        copy.wait()

    def serve(dz):
        block = grid[dz]
        sends = []
        for d in range(4):
            if dz == 0 and d == 0:
                continue
            lists = want[...] if d == 0 else asked[d]
            column = jnp.broadcast_to(lists[:, dz * 4 + d : dz * 4 + d + 1], (SLOT, FD))
            chosen = jnp.where(slot_lane == column, 1.0, 0.0).astype(BF16)
            got = nn(chosen, block).astype(BF16)
            if d == 0:
                rows[dz * 4] = got
            else:
                pick[dz, d] = got
                copy = remote(pick.at[dz, d], rows.at[dz * 4 + d], row_sem, (dz, d), x_of[d])
                copy.start()
                sends.append(copy)
        return sends

    sends = {0: serve(0)}

    mine.wait()
    for copy in msgs:
        copy.wait()
    lam = [jnp.sum(msg_in[j, pl.ds(DV, 16), :].astype(F32), axis=0, keepdims=True) for j in range(8)]
    grow = [jnp.exp(v) for v in lam]
    prefix, reach = [jnp.zeros((DV, FD), F32)], [jnp.zeros((1, FD), F32)]
    for j in range(8):
        prefix.append(grow[j] * prefix[-1] + msg_in[j, pl.ds(0, DV), :].astype(F32))
        reach.append(reach[-1] + lam[j])
    y_out[pl.ds(0, DV), :] = prefix[8]
    y_out[pl.ds(DV, 8), :] = jnp.broadcast_to(reach[8], (8, FD))
    y_copies = [remote(y_out, y_in.at[(4 - d) % 4], y_sem, (d,), y_of[d]) for d in range(1, 4)]
    for copy in y_copies:
        copy.start()

    up[0].wait()
    far_up.start()
    dn[0].wait()
    far_dn.start()

    for copy in y_copies:
        copy.wait()
    carry = jnp.zeros((DV, FD), F32)
    for d in range(1, 4):
        step = jnp.exp(y_in[d, pl.ds(DV, 1), :]) * carry + y_in[d, pl.ds(0, DV), :]
        carry = jnp.where(d >= 4 - y, step, carry)
    for j in range(8):
        ent_out[j] = (prefix[j] + jnp.exp(reach[j]) * carry).astype(BF16)
    own_entry = pltpu.make_async_copy(ent_out.at[i], ent.at[i], load_sem.at[8])
    own_entry.start()
    entries = [remote(ent_out.at[(i + d) % 8], ent.at[i], ent_sem, (d,), row_of[d]) for d in range(1, 8)]
    for copy in entries:
        copy.start()

    up[1].wait()
    sends[1] = serve(1)
    dn[1].wait()
    sends[3] = serve(3)

    loads[6].wait()
    own_entry.wait()
    for copy in entries:
        copy.wait()
    halves = []
    for h in range(H):
        carried = nt(ent[h], q_s[:, h * DK : (h + 1) * DK]) * (jnp.exp(cum[h : h + 1, :]) * scale)
        attended = inside[h] + carried
        halves.append(attended * lax.rsqrt(jnp.mean(attended * attended, axis=0, keepdims=True) + 1e-05))
    context = jnp.concatenate(
        [jnp.concatenate(halves[2 * c : 2 * c + 2], axis=0).T.astype(BF16) for c in range(E // FD)], axis=1
    )
    predicted = [nn(context, wp[k]).astype(BF16) for k in range(K)]

    @pl.when(has_prev)
    def _():
        fut_copy.wait_send()

    @pl.when(has_next)
    def _():
        fut_copy.wait_recv()
        halo_copy.wait_send()

    @pl.when(jnp.logical_not(has_next))
    def _():
        fut[...] = jnp.zeros_like(fut)

    inv_width = 1.0 / math.sqrt(E)
    valid_lane = jnp.where(lane[0:1, :] + m * FD < length, inv_width, 0.0)
    later = iota((16, FD), 0) + FD
    later_lane = iota((16, FD), 1)
    for k in range(K):
        here = jnp.where(sub == lane + (k + 1), nt(grid[0], predicted[k]), 0.0)
        ahead = jnp.where(later == later_lane + (k + 1), nt(fut[...], predicted[k]), 0.0)
        positive = jnp.sum(here, axis=0, keepdims=True) + jnp.sum(ahead, axis=0, keepdims=True)
        out_ref[0, k, 0:1, :] = positive * valid_lane

    negative = [[jnp.zeros((1, FD), F32) for _ in range(NNEG)] for _ in range(K)]

    def score(dz):
        start = 1 if dz == 0 else 0
        for d in range(start, 4):
            n = dz * 4 + d
            block = rows[n]
            found = [slot_rows + n * SLOT == spot[j] for j in range(NNEG)]
            for k in range(K):
                scores = nt(block, predicted[k])
                for j in range(NNEG):
                    negative[k][j] += jnp.sum(jnp.where(found[j], scores, 0.0), axis=0, keepdims=True)

    far_up.wait()
    far_dn.wait()
    sends[2] = serve(2)
    for dz in (0, 1, 3, 2):
        for copy in sends[dz]:
            copy.wait()
        score(dz)
    for k in range(K):
        for j in range(NNEG):
            out_ref[0, k, 1 + j : 2 + j, :] = negative[k][j] * valid_lane


def shards(raw, w_conv, w_query, w_key, w_pred, log_decay, lengths, neg_offset, neg_frame):
    aux = jnp.concatenate(
        [neg_offset[0].T, neg_frame[0].T, jnp.broadcast_to(lengths[0], (2, FD))], axis=0
    )
    hbm = pl.BlockSpec(memory_space=pl.ANY)
    dma = pltpu.SemaphoreType.DMA
    return pl.pallas_call(
        kernel,
        out_shape=jax.ShapeDtypeStruct((1, K, 1 + NNEG, FD), F32),
        in_specs=[hbm] * 7,
        out_specs=pl.BlockSpec(memory_space=pltpu.VMEM),
        scratch_shapes=[
            pltpu.VMEM((FD, FRAME_W), BF16),
            pltpu.VMEM((2 * FRAME_W, E), BF16),
            pltpu.VMEM((E, DA), BF16),
            pltpu.VMEM((E, DA), BF16),
            pltpu.VMEM((K, E, E), BF16),
            pltpu.VMEM((H, FD), F32),
            pltpu.VMEM((8, FD), I32),
            pltpu.VMEM((16, FRAME_W), BF16),
            pltpu.VMEM((16, E), BF16),
            pltpu.VMEM((SLOT, FD), I32),
            pltpu.VMEM((4, SLOT, FD), I32),
            pltpu.VMEM((4, FD, E), BF16),
            pltpu.VMEM((4, 4, SLOT, E), BF16),
            pltpu.VMEM((16, SLOT, E), BF16),
            pltpu.VMEM((H, MSG, FD), BF16),
            pltpu.VMEM((H, MSG, FD), BF16),
            pltpu.VMEM((YMSG, FD), F32),
            pltpu.VMEM((4, YMSG, FD), F32),
            pltpu.VMEM((H, DV, FD), BF16),
            pltpu.VMEM((H, DV, FD), BF16),
            pltpu.VMEM((FD, DA), BF16),
            pltpu.VMEM((H, DV, FD), F32),
            dma((9,)),
            dma((2,)),
            dma((2,)),
            dma((2, 4)),
            dma((2, 2, 2)),
            dma((2, 2)),
            dma((2, 4, 4)),
            dma((2, 8)),
            dma((2, 4)),
            dma((2, 8)),
        ],
        compiler_params=pltpu.CompilerParams(collective_id=0, has_side_effects=True),
    )(raw, w_conv, w_query, w_key, w_pred, log_decay, aux)


def solution(mesh):
    placed = (
        P("batch", "tm", None),
        P(),
        P(),
        P(),
        P(),
        P("batch", None, "tm"),
        P("batch"),
        P("batch", "tm", None),
        P("batch", "tm", None),
    )
    return jax.shard_map(
        shards, mesh=mesh, in_specs=placed, out_specs=P("batch", None, None, "tm"), check_vma=False
    )
```

```python
import functools
import math

import jax
import jax.numpy as jnp
from jax import lax
from jax.experimental import pallas as pl
from jax.experimental.pallas import tpu as pltpu
from jax.sharding import PartitionSpec as P

MESH = pl.DeviceIdType.MESH
F32, BF16, I32 = jnp.float32, jnp.bfloat16, jnp.int32
FD, E, DA, H, FRAME_W, K, NNEG = 128, 512, 1024, 8, 640, 2, 3
DK, DV = DA // H, E // H
SLOT = 48
CHUNK = FD // 4
MSG = DV + 16
YMSG = DV + 8


def nt(a, b):
    return lax.dot_general(a, b, (((1,), (1,)), ((), ())), preferred_element_type=F32)


def nn(a, b):
    return jnp.dot(a, b, preferred_element_type=F32)


def iota(shape, axis):
    return lax.broadcasted_iota(I32, shape, axis)


def kernel(
    raw_hbm, wc_hbm, wq_hbm, wk_hbm, wp_hbm, ld_hbm, off_hbm, frm_hbm, len_ref, out_ref,
    raw, wc, wq, wk, wp, ld, off, frm, halo, fut, want, asked, grid, pick, rows,
    st_out, st_in, msg_out, msg_in, y_out, y_in, ent_out, ent_in, ent_pair, ent, q_s, inside,
    load_sem, halo_sem, fut_sem, ask_sem, near_sem, far_sem, row_sem, pair_sem, msg_sem, y_sem, ent_sem,
):
    b, m = lax.axis_index("batch"), lax.axis_index("tm")
    zh, x = b // 4, b % 4
    y, zl, c = m // 8, (m // 2) % 4, m % 2

    def remote(src, dst, sems, index, dev):
        return pltpu.make_async_remote_copy(
            src_ref=src, dst_ref=dst, send_sem=sems.at[(0, *index)], recv_sem=sems.at[(1, *index)],
            device_id=dev, device_id_type=MESH,
        )

    loads = [
        pltpu.make_async_copy(src, dst, load_sem.at[n])
        for n, (src, dst) in enumerate(
            [(raw_hbm.at[0], raw), (wc_hbm, wc), (off_hbm, off), (frm_hbm, frm), (ld_hbm.at[0], ld),
             (wk_hbm, wk), (wq_hbm, wq), (wp_hbm, wp)]
        )
    ]
    loads[0].start()
    loads[1].start()

    z_up, z_dn = (((zh + 1) % 4) * 4 + x, m), (((zh + 3) % 4) * 4 + x, m)
    x_of = [(zh * 4 + (x + d) % 4, m) for d in range(4)]
    pair = (b, m + 1 - 2 * c)
    row_of = [(b, y * 8 + ((zl + d) % 4) * 2 + c) for d in range(4)]
    y_of = [(b, ((y + d) % 4) * 8 + zl * 2 + c) for d in range(4)]
    nxt, prv = (b, jnp.minimum(m + 1, 31)), (b, jnp.maximum(m - 1, 0))
    has_next, has_prev = m < 31, m > 0
    edge_next = jnp.logical_and(c == 1, has_next)
    edge_prev = jnp.logical_and(c == 0, has_prev)

    barrier = pltpu.get_barrier_semaphore()
    for dev in [z_up, z_dn] + x_of[1:] + y_of[1:] + row_of[1:] + [pair]:
        pl.semaphore_signal(barrier, inc=1, device_id=dev, device_id_type=MESH)

    @pl.when(edge_next)
    def _():
        pl.semaphore_signal(barrier, inc=1, device_id=nxt, device_id_type=MESH)

    @pl.when(edge_prev)
    def _():
        pl.semaphore_signal(barrier, inc=1, device_id=prv, device_id_type=MESH)

    for load in loads[2:]:
        load.start()

    lane = iota((FD, FD), 1)
    sub = iota((FD, FD), 0)
    length = len_ref[0]
    valid_rows = jnp.where(sub + m * FD < length, 1.0, 0.0)
    valid_rows = jnp.concatenate([valid_rows] * 4, axis=1)

    def encode(hidden, valid):
        u = jax.nn.gelu(hidden)
        return (u * lax.rsqrt(jnp.mean(u * u, axis=-1, keepdims=True) + 1e-05) * valid).astype(BF16)

    loads[0].wait()
    loads[1].wait()
    before = pltpu.roll(nn(raw[...], wc[:FRAME_W, :]), 1, 0)
    now = nn(raw[...], wc[FRAME_W:, :])
    enc = encode(now + before, valid_rows)
    grid[0] = enc

    def part(n):
        return pl.ds(n * CHUNK, CHUNK)

    up_order, dn_order = (3, 2, 1, 0), (1, 0, 3, 2)
    up = [remote(grid.at[0, part(n), :], grid.at[1, part(n), :], near_sem, (0, n), z_up) for n in range(4)]
    dn = [remote(grid.at[0, part(n), :], grid.at[3, part(n), :], near_sem, (1, n), z_dn) for n in range(4)]
    far_up = [remote(grid.at[1, part(n), :], grid.at[2, part(n), :], far_sem, (0, n % 2), z_up) for n in (3, 2)]
    far_dn = [remote(grid.at[3, part(n), :], grid.at[2, part(n), :], far_sem, (1, n % 2), z_dn) for n in (1, 0)]
    halo_copy = remote(raw.at[pl.ds(FD - 16, 16), :], halo, halo_sem, (), nxt)
    fut_copy = remote(grid.at[0, pl.ds(0, 16), :], fut, fut_sem, (), prv)
    asks = [remote(want, asked.at[d], ask_sem, (d,), x_of[(4 - d) % 4]) for d in range(1, 4)]

    edges = jnp.where(c == 1, jnp.where(has_next, 1, 0), jnp.where(has_prev, 1, 0))
    pl.semaphore_wait(barrier, 12 + edges)

    @pl.when(has_next)
    def _():
        halo_copy.start()

    up[3].start()
    dn[1].start()

    loads[2].wait()
    loads[3].wait()
    rel_j, frame_j = [], []
    for j in range(NNEG):
        group = (b + off[j] + 1) & 15
        rel_j.append((((zh - (group >> 2)) & 3) << 2) | ((x - (group & 3)) & 3))
        frame_j.append(frm[j])
    rel_rows = iota((16, FD), 0)
    hit = [jnp.where(rel_rows == rel_j[j], 1, 0) for j in range(NNEG)]
    named = hit[0] + hit[1] + hit[2]
    frame_of = hit[0] * frame_j[0] + hit[1] * frame_j[1] + hit[2] * frame_j[2]
    upto = jnp.where(sub <= lane, 1.0, 0.0).astype(BF16)
    rank = nn(named.astype(F32).astype(BF16), upto).astype(I32) - 1
    spot = [jnp.sum(hit[j] * (rel_rows * SLOT + rank), axis=0, keepdims=True) for j in range(NNEG)]
    code = jnp.where(named > 0, rank, -1)
    slot_rows = iota((SLOT, FD), 0)
    slot_lane = iota((SLOT, FD), 1)
    wanted = jnp.zeros((SLOT, FD), I32)
    for r in range(1, 16):
        column = jnp.sum(
            jnp.where(slot_rows == code[r : r + 1, :], frame_of[r : r + 1, :].astype(F32), 0.0), axis=1, keepdims=True
        )
        wanted = jnp.where(slot_lane == r, column.astype(I32), wanted)
    want[...] = wanted
    for copy in asks:
        copy.start()

    loads[4].wait()
    cum = ld[...]
    lane8 = iota((H, FD), 1)
    for shift in (1, 2, 4, 8, 16, 32, 64):
        cum = cum + jnp.where(lane8 >= shift, pltpu.roll(cum, shift, 1), 0.0)
    cum_col = jnp.concatenate([cum, jnp.zeros((FD - H, FD), F32)], axis=0).T
    total = jnp.sum(jnp.where(lane8 == FD - 1, cum, 0.0), axis=1, keepdims=True)
    total_row = jnp.broadcast_to(total, (H, FD))

    @pl.when(has_prev)
    def _():
        halo_copy.wait_recv()

    @pl.when(jnp.logical_not(has_prev))
    def _():
        halo[...] = jnp.zeros_like(halo)

    edge = nn(halo[...], wc[:FRAME_W, :])
    first = iota((16, E), 0) == 0
    top = encode(
        now[:16, :] + jnp.where(first, jnp.broadcast_to(edge[15:16, :], (16, E)), before[:16, :]), valid_rows[:16, :]
    )
    grid[0, pl.ds(0, 16), :] = top
    enc = jnp.concatenate([top, enc[16:, :]], axis=0)
    up[2].start()
    dn[0].start()

    @pl.when(has_prev)
    def _():
        fut_copy.start()

    loads[5].wait()
    enc_t = [enc[:, n * FD : (n + 1) * FD].T for n in range(E // FD)]
    value_t = [enc_t[h // 2][(h % 2) * DV : (h % 2 + 1) * DV, :] for h in range(H)]
    keys = nn(enc, wk[...]).astype(BF16)
    for h in range(H):
        key = keys[:, h * DK : (h + 1) * DK]
        to_end = jnp.exp(total_row[h : h + 1, :] - jnp.broadcast_to(cum_col[:, h : h + 1], (FD, FD)))
        weighted = (key.astype(F32) * to_end).astype(BF16)
        st_out[h, pl.ds(0, DV), :] = nn(value_t[h], weighted)
        st_out[h, pl.ds(DV, 8), :] = jnp.broadcast_to(total_row[h : h + 1, :], (8, FD))
    pair_copy = remote(st_out.at[pl.ds(4 - 4 * c, 4)], st_in, pair_sem, (0,), pair)
    pair_copy.start()

    loads[6].wait()
    queries = nn(enc, wq[...]).astype(BF16)
    q_s[...] = queries

    def core_states(n):
        own, other = st_out[4 * c + n], st_in[n]
        return jnp.where(c == 0, own, other), jnp.where(c == 0, other, own)

    pair_copy.wait()
    rows16 = iota((16, FD), 0)
    for n in range(4):
        early, late = core_states(n)
        joined = jnp.exp(late[DV : DV + 1, :]) * early[:DV, :] + late[:DV, :]
        whole = early[DV : DV + 1, :] + late[DV : DV + 1, :]
        hi = whole.astype(BF16).astype(F32)
        mid = (whole - hi).astype(BF16).astype(F32)
        lo = whole - hi - mid
        pieces = jnp.where(rows16 == 0, hi, jnp.where(rows16 == 1, mid, jnp.where(rows16 == 2, lo, 0.0)))
        msg_out[n, pl.ds(0, DV), :] = joined.astype(BF16)
        msg_out[n, pl.ds(DV, 16), :] = pieces.astype(BF16)
    msgs = [remote(msg_out.at[(zl + d) % 4], msg_in.at[zl], msg_sem, (d,), row_of[d]) for d in range(1, 4)]
    for copy in msgs:
        copy.start()
    msg_in[zl] = msg_out[zl]
    for n in range(2, 4):
        up[up_order[n]].start()
        dn[dn_order[n]].start()

    scale = 1.0 / math.sqrt(DK)
    for h in range(H):
        key = keys[:, h * DK : (h + 1) * DK]
        query = queries[:, h * DK : (h + 1) * DK]
        gap = cum[h : h + 1, :] - jnp.broadcast_to(cum_col[:, h : h + 1], (FD, FD))
        weight = jnp.where(sub <= lane, jnp.exp(jnp.minimum(gap, 0.0)), 0.0)
        probs_t = (nt(key, query) * weight * scale).astype(BF16)
        inside[h] = nn(value_t[h], probs_t)

    for copy in asks:
        copy.wait()

    def serve(dz):
        block = grid[dz]
        sends = []
        for d in range(4):
            if dz == 0 and d == 0:
                continue
            lists = want[...] if d == 0 else asked[d]
            column = jnp.broadcast_to(lists[:, dz * 4 + d : dz * 4 + d + 1], (SLOT, FD))
            chosen = jnp.where(slot_lane == column, 1.0, 0.0).astype(BF16)
            got = nn(chosen, block).astype(BF16)
            if d == 0:
                rows[dz * 4] = got
            else:
                pick[dz, d] = got
                copy = remote(pick.at[dz, d], rows.at[dz * 4 + d], row_sem, (dz, d), x_of[d])
                copy.start()
                sends.append(copy)
        return sends

    sends = {0: serve(0)}

    up[3].wait()
    far_up[0].start()
    dn[1].wait()
    far_dn[0].start()

    for copy in msgs:
        copy.wait()
    lam = [jnp.sum(msg_in[n, pl.ds(DV, 16), :].astype(F32), axis=0, keepdims=True) for n in range(4)]
    prefix, reach = [jnp.zeros((DV, FD), F32)], [jnp.zeros((1, FD), F32)]
    for n in range(4):
        prefix.append(jnp.exp(lam[n]) * prefix[-1] + msg_in[n, pl.ds(0, DV), :].astype(F32))
        reach.append(reach[-1] + lam[n])
    y_out[pl.ds(0, DV), :] = prefix[4]
    y_out[pl.ds(DV, 8), :] = jnp.broadcast_to(reach[4], (8, FD))
    y_copies = [remote(y_out, y_in.at[(4 - d) % 4], y_sem, (d,), y_of[d]) for d in range(1, 4)]
    for copy in y_copies:
        copy.start()

    up[2].wait()
    far_up[1].start()
    dn[0].wait()
    far_dn[1].start()

    for copy in y_copies:
        copy.wait()
    carry = jnp.zeros((DV, FD), F32)
    for d in range(1, 4):
        step = jnp.exp(y_in[d, pl.ds(DV, 1), :]) * carry + y_in[d, pl.ds(0, DV), :]
        carry = jnp.where(d >= 4 - y, step, carry)
    for n in range(4):
        ent_out[n] = (prefix[n] + jnp.exp(reach[n]) * carry).astype(BF16)
    entries = [remote(ent_out.at[(zl + d) % 4], ent_in.at[zl], ent_sem, (d,), row_of[d]) for d in range(1, 4)]
    for copy in entries:
        copy.start()
    ent_in[zl] = ent_out[zl]

    for n in range(2):
        up[n].wait()
    sends[1] = serve(1)
    for n in range(2, 4):
        dn[n].wait()
    sends[3] = serve(3)

    for copy in entries:
        copy.wait()
    for n in range(4):
        early, _ = core_states(n)
        at_first = ent_in[n].astype(F32)
        at_second = jnp.exp(early[DV : DV + 1, :]) * at_first + early[:DV, :]
        ent[4 * c + n] = jnp.where(c == 0, at_first, at_second).astype(BF16)
        ent_pair[n] = jnp.where(c == 0, at_second, at_first).astype(BF16)
    back_copy = remote(ent_pair, ent.at[pl.ds(4 * c, 4)], pair_sem, (1,), pair)
    back_copy.start()
    loads[7].wait()
    back_copy.wait()
    halves = []
    for h in range(H):
        carried = nt(ent[h], q_s[:, h * DK : (h + 1) * DK]) * (jnp.exp(cum[h : h + 1, :]) * scale)
        attended = inside[h] + carried
        halves.append(attended * lax.rsqrt(jnp.mean(attended * attended, axis=0, keepdims=True) + 1e-05))
    context = jnp.concatenate(
        [jnp.concatenate(halves[2 * n : 2 * n + 2], axis=0).T.astype(BF16) for n in range(E // FD)], axis=1
    )
    predicted = [nn(context, wp[k]).astype(BF16) for k in range(K)]

    @pl.when(has_prev)
    def _():
        fut_copy.wait_send()

    @pl.when(has_next)
    def _():
        fut_copy.wait_recv()
        halo_copy.wait_send()

    @pl.when(jnp.logical_not(has_next))
    def _():
        fut[...] = jnp.zeros_like(fut)

    for copy in far_up + far_dn:
        copy.wait()
    sends[2] = serve(2)

    inv_width = 1.0 / math.sqrt(E)
    valid_lane = jnp.where(lane[0:1, :] + m * FD < length, inv_width, 0.0)
    later = iota((16, FD), 0) + FD
    later_lane = iota((16, FD), 1)
    for k in range(K):
        here = jnp.where(sub == lane + (k + 1), nt(grid[0], predicted[k]), 0.0)
        ahead = jnp.where(later == later_lane + (k + 1), nt(fut[...], predicted[k]), 0.0)
        positive = jnp.sum(here, axis=0, keepdims=True) + jnp.sum(ahead, axis=0, keepdims=True)
        out_ref[0, k, 0:1, :] = positive * valid_lane

    negative = [[jnp.zeros((1, FD), F32) for _ in range(NNEG)] for _ in range(K)]

    def score(dz):
        start = 1 if dz == 0 else 0
        for d in range(start, 4):
            n = dz * 4 + d
            block = rows[n]
            found = [slot_rows + n * SLOT == spot[j] for j in range(NNEG)]
            for k in range(K):
                scores = nt(block, predicted[k])
                for j in range(NNEG):
                    negative[k][j] += jnp.sum(jnp.where(found[j], scores, 0.0), axis=0, keepdims=True)

    for dz in (0, 1, 3, 2):
        for copy in sends[dz]:
            copy.wait()
        score(dz)
    for k in range(K):
        for j in range(NNEG):
            out_ref[0, k, 1 + j : 2 + j, :] = negative[k][j] * valid_lane


def shards(raw, w_conv, w_query, w_key, w_pred, log_decay, lengths, neg_offset, neg_frame):
    hbm = pl.BlockSpec(memory_space=pl.ANY)
    dma = pltpu.SemaphoreType.DMA
    return pl.pallas_call(
        kernel,
        out_shape=jax.ShapeDtypeStruct((1, K, 1 + NNEG, FD), F32),
        in_specs=[hbm] * 8 + [pl.BlockSpec(memory_space=pltpu.SMEM)],
        out_specs=pl.BlockSpec(memory_space=pltpu.VMEM),
        scratch_shapes=[
            pltpu.VMEM((FD, FRAME_W), BF16),
            pltpu.VMEM((2 * FRAME_W, E), BF16),
            pltpu.VMEM((E, DA), BF16),
            pltpu.VMEM((E, DA), BF16),
            pltpu.VMEM((K, E, E), BF16),
            pltpu.VMEM((H, FD), F32),
            pltpu.VMEM((NNEG, 1, FD), I32),
            pltpu.VMEM((NNEG, 1, FD), I32),
            pltpu.VMEM((16, FRAME_W), BF16),
            pltpu.VMEM((16, E), BF16),
            pltpu.VMEM((SLOT, FD), I32),
            pltpu.VMEM((4, SLOT, FD), I32),
            pltpu.VMEM((4, FD, E), BF16),
            pltpu.VMEM((4, 4, SLOT, E), BF16),
            pltpu.VMEM((16, SLOT, E), BF16),
            pltpu.VMEM((H, DV + 8, FD), F32),
            pltpu.VMEM((4, DV + 8, FD), F32),
            pltpu.VMEM((4, MSG, FD), BF16),
            pltpu.VMEM((4, MSG, FD), BF16),
            pltpu.VMEM((YMSG, FD), F32),
            pltpu.VMEM((4, YMSG, FD), F32),
            pltpu.VMEM((4, DV, FD), BF16),
            pltpu.VMEM((4, DV, FD), BF16),
            pltpu.VMEM((4, DV, FD), BF16),
            pltpu.VMEM((H, DV, FD), BF16),
            pltpu.VMEM((FD, DA), BF16),
            pltpu.VMEM((H, DV, FD), F32),
            dma((8,)),
            dma((2,)),
            dma((2,)),
            dma((2, 4)),
            dma((2, 2, 4)),
            dma((2, 2, 2)),
            dma((2, 4, 4)),
            dma((2, 2)),
            dma((2, 4)),
            dma((2, 4)),
            dma((2, 4)),
        ],
        compiler_params=pltpu.CompilerParams(collective_id=0, has_side_effects=True),
    )(
        raw, w_conv, w_query, w_key, w_pred, log_decay,
        jnp.transpose(neg_offset, (2, 0, 1)), jnp.transpose(neg_frame, (2, 0, 1)), lengths,
    )


def solution(mesh):
    placed = (
        P("batch", "tm", None),
        P(),
        P(),
        P(),
        P(),
        P("batch", None, "tm"),
        P("batch"),
        P("batch", "tm", None),
        P("batch", "tm", None),
    )
    return jax.shard_map(
        shards, mesh=mesh, in_specs=placed, out_specs=P("batch", None, None, "tm"), check_vma=False
    )
```

```python
import functools
import math

import jax
import jax.numpy as jnp
from jax import lax
from jax.experimental import pallas as pl
from jax.experimental.pallas import tpu as pltpu
from jax.sharding import PartitionSpec as P

MESH = pl.DeviceIdType.MESH
F32, BF16, I32 = jnp.float32, jnp.bfloat16, jnp.int32
FD, E, DA, H, FRAME_W, K, NNEG = 128, 512, 1024, 8, 640, 2, 3
DK, DV = DA // H, E // H
SLOT, PAD = 40, 48
CHUNK = FD // 4
MSG = DV + 16
YMSG = DV + 8


def nt(a, b):
    return lax.dot_general(a, b, (((1,), (1,)), ((), ())), preferred_element_type=F32)


def nn(a, b):
    return jnp.dot(a, b, preferred_element_type=F32)


def iota(shape, axis):
    return lax.broadcasted_iota(I32, shape, axis)


def kernel(
    raw_hbm, wc_hbm, wq_hbm, wk_hbm, wp_hbm, ld_hbm, off_hbm, frm_hbm, len_ref, out_ref,
    raw, wc, wq, wk, wp, ld, off, frm, halo, fut, want, asked, grid, pick, rows,
    chosen, st_out, st_in, msg_out, msg_in, y_out, y_in, ent_out, ent_in, ent_pair, ent, q_s, inside,
    load_sem, halo_sem, fut_sem, ask_sem, near_sem, far_sem, row_sem, pair_sem, msg_sem, y_sem, ent_sem,
):
    b, m = lax.axis_index("batch"), lax.axis_index("tm")
    zh, x = b // 4, b % 4
    y, zl, c = m // 8, (m // 2) % 4, m % 2

    def remote(src, dst, sems, out, back, dev):
        return pltpu.make_async_remote_copy(
            src_ref=src, dst_ref=dst, send_sem=sems.at[out], recv_sem=sems.at[back],
            device_id=dev, device_id_type=MESH,
        )

    loads = [
        pltpu.make_async_copy(src, dst, load_sem.at[n])
        for n, (src, dst) in enumerate(
            [(raw_hbm.at[0], raw), (wc_hbm, wc), (off_hbm, off), (frm_hbm, frm), (ld_hbm.at[0], ld),
             (wk_hbm, wk), (wq_hbm, wq), (wp_hbm, wp)]
        )
    ]
    loads[0].start()
    loads[1].start()

    z_up, z_dn = (((zh + 1) % 4) * 4 + x, m), (((zh + 3) % 4) * 4 + x, m)
    x_of = [(zh * 4 + (x + d) % 4, m) for d in range(4)]
    pair = (b, m + 1 - 2 * c)
    row_of = [(b, y * 8 + ((zl + d) % 4) * 2 + c) for d in range(4)]
    y_of = [(b, ((y + d) % 4) * 8 + zl * 2 + c) for d in range(4)]
    nxt, prv = (b, jnp.minimum(m + 1, 31)), (b, jnp.maximum(m - 1, 0))
    has_next, has_prev = m < 31, m > 0
    edge_next = jnp.logical_and(c == 1, has_next)
    edge_prev = jnp.logical_and(c == 0, has_prev)

    barrier = pltpu.get_barrier_semaphore()
    for dev in [z_up, z_dn] + x_of[1:] + y_of[1:] + row_of[1:] + [pair]:
        pl.semaphore_signal(barrier, inc=1, device_id=dev, device_id_type=MESH)

    @pl.when(edge_next)
    def _():
        pl.semaphore_signal(barrier, inc=1, device_id=nxt, device_id_type=MESH)

    @pl.when(edge_prev)
    def _():
        pl.semaphore_signal(barrier, inc=1, device_id=prv, device_id_type=MESH)

    for load in loads[2:]:
        load.start()

    lane = iota((FD, FD), 1)
    sub = iota((FD, FD), 0)
    length = len_ref[0]
    valid_rows = jnp.where(sub + m * FD < length, 1.0, 0.0)
    valid_rows = jnp.concatenate([valid_rows] * 4, axis=1)

    def encode(hidden, valid):
        u = jax.nn.gelu(hidden)
        return (u * lax.rsqrt(jnp.mean(u * u, axis=-1, keepdims=True) + 1e-05) * valid).astype(BF16)

    loads[0].wait()
    loads[1].wait()
    before = pltpu.roll(nn(raw[...], wc[:FRAME_W, :]), 1, 0)
    now = nn(raw[...], wc[FRAME_W:, :])
    enc = encode(now + before, valid_rows)
    grid[0] = enc

    def part(n):
        return pl.ds(n * CHUNK, CHUNK)

    low, high = pl.ds(0, 2 * CHUNK), pl.ds(2 * CHUNK, 2 * CHUNK)
    up = [remote(grid.at[0, part(n), :], grid.at[1, part(n), :], near_sem, 0, 2 + max(n - 1, 0), z_up) for n in range(4)]
    dn = [remote(grid.at[0, part(n), :], grid.at[3, part(n), :], near_sem, 1, 5 + min(n, 2), z_dn) for n in range(4)]
    up_all, dn_all = remote(grid.at[0], grid.at[1], near_sem, 0, 2, z_up), remote(grid.at[0], grid.at[3], near_sem, 1, 7, z_dn)
    up_rest = remote(grid.at[0, low, :], grid.at[1, low, :], near_sem, 0, 2, z_up)
    dn_rest = remote(grid.at[0, high, :], grid.at[3, high, :], near_sem, 1, 7, z_dn)
    far_up = [remote(grid.at[1, part(n), :], grid.at[2, part(n), :], far_sem, 0, 1, z_up) for n in (3, 2)]
    far_dn = [remote(grid.at[3, part(n), :], grid.at[2, part(n), :], far_sem, 2, 3, z_dn) for n in (1, 0)]
    far_all = [
        remote(grid.at[1, high, :], grid.at[2, high, :], far_sem, 0, 1, z_up),
        remote(grid.at[3, low, :], grid.at[2, low, :], far_sem, 2, 3, z_dn),
    ]
    halo_copy = remote(raw.at[pl.ds(FD - 16, 16), :], halo, halo_sem, 0, 1, nxt)
    fut_copy = remote(grid.at[0, pl.ds(0, 16), :], fut, fut_sem, 0, 1, prv)
    asks = [remote(want, asked.at[d], ask_sem, 0, 1, x_of[(4 - d) % 4]) for d in range(1, 4)]
    asks_all = remote(asked.at[pl.ds(1, 3)], asked.at[pl.ds(1, 3)], ask_sem, 0, 1, x_of[1])

    edges = jnp.where(c == 1, jnp.where(has_next, 1, 0), jnp.where(has_prev, 1, 0))
    pl.semaphore_wait(barrier, 12 + edges)

    @pl.when(has_next)
    def _():
        halo_copy.start()

    up[3].start()
    dn[1].start()

    loads[2].wait()
    loads[3].wait()
    rel_j, frame_j = [], []
    for j in range(NNEG):
        group = (b + off[j] + 1) & 15
        rel_j.append((((zh - (group >> 2)) & 3) << 2) | ((x - (group & 3)) & 3))
        frame_j.append(frm[j])
    rel_rows = iota((16, FD), 0)
    hit = [jnp.where(rel_rows == rel_j[j], 1, 0) for j in range(NNEG)]
    named = hit[0] + hit[1] + hit[2]
    frame_of = hit[0] * frame_j[0] + hit[1] * frame_j[1] + hit[2] * frame_j[2]
    upto = jnp.where(sub <= lane, 1.0, 0.0).astype(BF16)
    rank = nn(named.astype(F32).astype(BF16), upto).astype(I32) - 1
    spot = [jnp.sum(hit[j] * (rel_rows * SLOT + rank), axis=0, keepdims=True) for j in range(NNEG)]
    code = jnp.where(named > 0, rank, -1)
    slot_rows = iota((SLOT, FD), 0)
    pad_rows = iota((PAD, FD), 0)
    pad_lane = iota((PAD, FD), 1)
    wanted = jnp.zeros((PAD, FD), I32)
    for r in range(1, 16):
        column = jnp.sum(
            jnp.where(pad_rows == code[r : r + 1, :], frame_of[r : r + 1, :].astype(F32), 0.0), axis=1, keepdims=True
        )
        wanted = jnp.where(pad_lane == r, column.astype(I32), wanted)
    want[...] = wanted
    for copy in asks:
        copy.start()

    loads[4].wait()
    cum = ld[...]
    lane8 = iota((H, FD), 1)
    for shift in (1, 2, 4, 8, 16, 32, 64):
        cum = cum + jnp.where(lane8 >= shift, pltpu.roll(cum, shift, 1), 0.0)
    cum_col = jnp.concatenate([cum, jnp.zeros((FD - H, FD), F32)], axis=0).T
    total = jnp.sum(jnp.where(lane8 == FD - 1, cum, 0.0), axis=1, keepdims=True)
    total_row = jnp.broadcast_to(total, (H, FD))

    @pl.when(has_prev)
    def _():
        halo_copy.wait_recv()

    @pl.when(jnp.logical_not(has_prev))
    def _():
        halo[...] = jnp.zeros_like(halo)

    edge = nn(halo[...], wc[:FRAME_W, :])
    first = iota((16, E), 0) == 0
    top = encode(
        now[:16, :] + jnp.where(first, jnp.broadcast_to(edge[15:16, :], (16, E)), before[:16, :]), valid_rows[:16, :]
    )
    grid[0, pl.ds(0, 16), :] = top
    enc = jnp.concatenate([top, enc[16:, :]], axis=0)
    up[2].start()
    dn[0].start()

    @pl.when(has_prev)
    def _():
        fut_copy.start()

    loads[5].wait()
    enc_t = [enc[:, n * FD : (n + 1) * FD].T for n in range(E // FD)]
    value_t = [enc_t[h // 2][(h % 2) * DV : (h % 2 + 1) * DV, :] for h in range(H)]
    keys = nn(enc, wk[...]).astype(BF16)
    for h in range(H):
        key = keys[:, h * DK : (h + 1) * DK]
        to_end = jnp.exp(total_row[h : h + 1, :] - jnp.broadcast_to(cum_col[:, h : h + 1], (FD, FD)))
        weighted = (key.astype(F32) * to_end).astype(BF16)
        st_out[h, pl.ds(0, DV), :] = nn(value_t[h], weighted)
        st_out[h, pl.ds(DV, 8), :] = jnp.broadcast_to(total_row[h : h + 1, :], (8, FD))
    pair_copy = remote(st_out.at[pl.ds(4 - 4 * c, 4)], st_in, pair_sem, 0, 1, pair)
    pair_copy.start()

    loads[6].wait()
    queries = nn(enc, wq[...]).astype(BF16)
    q_s[...] = queries

    def core_states(n):
        own, other = st_out[4 * c + n], st_in[n]
        return jnp.where(c == 0, own, other), jnp.where(c == 0, other, own)

    pair_copy.wait()
    rows16 = iota((16, FD), 0)
    for n in range(4):
        early, late = core_states(n)
        joined = jnp.exp(late[DV : DV + 1, :]) * early[:DV, :] + late[:DV, :]
        whole = early[DV : DV + 1, :] + late[DV : DV + 1, :]
        hi = whole.astype(BF16).astype(F32)
        mid = (whole - hi).astype(BF16).astype(F32)
        lo = whole - hi - mid
        pieces = jnp.where(rows16 == 0, hi, jnp.where(rows16 == 1, mid, jnp.where(rows16 == 2, lo, 0.0)))
        msg_out[n, pl.ds(0, DV), :] = joined.astype(BF16)
        msg_out[n, pl.ds(DV, 16), :] = pieces.astype(BF16)
    msgs = [remote(msg_out.at[(zl + d) % 4], msg_in.at[zl], msg_sem, 0, 1, row_of[d]) for d in range(1, 4)]
    msgs_all = remote(msg_out.at[pl.ds(0, 3)], msg_in.at[pl.ds(0, 3)], msg_sem, 0, 1, row_of[1])
    for copy in msgs:
        copy.start()
    msg_in[zl] = msg_out[zl]
    up[1].start()
    dn[3].start()
    up[0].start()
    dn[2].start()

    scale = 1.0 / math.sqrt(DK)
    for h in range(H):
        key = keys[:, h * DK : (h + 1) * DK]
        query = queries[:, h * DK : (h + 1) * DK]
        gap = cum[h : h + 1, :] - jnp.broadcast_to(cum_col[:, h : h + 1], (FD, FD))
        weight = jnp.where(sub <= lane, jnp.exp(jnp.minimum(gap, 0.0)), 0.0)
        probs_t = (nt(key, query) * weight * scale).astype(BF16)
        inside[h] = nn(value_t[h], probs_t)

    asks_all.wait()

    for dz in range(4):
        for d in range(4):
            lists = want[...] if d == 0 else asked[d]
            column = jnp.broadcast_to(lists[:, dz * 4 + d : dz * 4 + d + 1], (PAD, FD))
            chosen[dz, pl.ds(d * PAD, PAD), :] = jnp.where(pad_lane == column, 1.0, 0.0).astype(BF16)

    def serve(dz):
        got = nn(chosen[dz], grid[dz]).astype(BF16)
        for d in (2, 1, 3):
            pick[dz, d] = got[d * PAD : d * PAD + SLOT, :]
            remote(pick.at[dz, d], rows.at[dz * 4 + d], row_sem, dz, 4 + dz, x_of[d]).start()
        if dz > 0:
            rows[dz * 4] = got[:SLOT, :]
        return remote(pick.at[dz, pl.ds(1, 3)], rows.at[pl.ds(dz * 4 + 1, 3)], row_sem, dz, 4 + dz, x_of[1])

    sends = {0: serve(0)}

    up[3].wait_recv()
    far_up[0].start()
    dn[1].wait_recv()
    far_dn[0].start()

    msgs_all.wait()
    lam = [jnp.sum(msg_in[n, pl.ds(DV, 16), :].astype(F32), axis=0, keepdims=True) for n in range(4)]
    prefix, reach = [jnp.zeros((DV, FD), F32)], [jnp.zeros((1, FD), F32)]
    for n in range(4):
        prefix.append(jnp.exp(lam[n]) * prefix[-1] + msg_in[n, pl.ds(0, DV), :].astype(F32))
        reach.append(reach[-1] + lam[n])
    y_out[pl.ds(0, DV), :] = prefix[4]
    y_out[pl.ds(DV, 8), :] = jnp.broadcast_to(reach[4], (8, FD))
    y_copies = [remote(y_out, y_in.at[(4 - d) % 4], y_sem, 0, 1, y_of[d]) for d in range(1, 4)]
    y_all = remote(y_in.at[pl.ds(1, 3)], y_in.at[pl.ds(1, 3)], y_sem, 0, 1, y_of[1])
    for copy in y_copies:
        copy.start()
    up[2].wait_recv()
    far_up[1].start()
    dn[0].wait_recv()
    far_dn[1].start()

    y_all.wait()
    carry = jnp.zeros((DV, FD), F32)
    for d in range(1, 4):
        step = jnp.exp(y_in[d, pl.ds(DV, 1), :]) * carry + y_in[d, pl.ds(0, DV), :]
        carry = jnp.where(d >= 4 - y, step, carry)
    for n in range(4):
        ent_out[n] = (prefix[n] + jnp.exp(reach[n]) * carry).astype(BF16)
    entries = [remote(ent_out.at[(zl + d) % 4], ent_in.at[zl], ent_sem, 0, 1, row_of[d]) for d in range(1, 4)]
    entries_all = remote(ent_out.at[pl.ds(0, 3)], ent_in.at[pl.ds(0, 3)], ent_sem, 0, 1, row_of[1])
    for copy in entries:
        copy.start()
    ent_in[zl] = ent_out[zl]

    up_rest.wait_recv()
    sends[1] = serve(1)
    dn_rest.wait_recv()
    sends[3] = serve(3)
    for copy in far_all:
        copy.wait()
    sends[2] = serve(2)
    entries_all.wait()
    for n in range(4):
        early, _ = core_states(n)
        at_first = ent_in[n].astype(F32)
        at_second = jnp.exp(early[DV : DV + 1, :]) * at_first + early[:DV, :]
        ent[4 * c + n] = jnp.where(c == 0, at_first, at_second).astype(BF16)
        ent_pair[n] = jnp.where(c == 0, at_second, at_first).astype(BF16)
    back_copy = remote(ent_pair, ent.at[pl.ds(4 * c, 4)], pair_sem, 2, 3, pair)
    back_copy.start()
    loads[7].wait()
    back_copy.wait()
    halves = []
    for h in range(H):
        carried = nt(ent[h], q_s[:, h * DK : (h + 1) * DK]) * (jnp.exp(cum[h : h + 1, :]) * scale)
        attended = inside[h] + carried
        halves.append(attended * lax.rsqrt(jnp.mean(attended * attended, axis=0, keepdims=True) + 1e-05))
    context = jnp.concatenate(
        [jnp.concatenate(halves[2 * n : 2 * n + 2], axis=0).T.astype(BF16) for n in range(E // FD)], axis=1
    )
    predicted = [nn(context, wp[k]).astype(BF16) for k in range(K)]

    @pl.when(has_prev)
    def _():
        fut_copy.wait_send()

    @pl.when(has_next)
    def _():
        fut_copy.wait_recv()
        halo_copy.wait_send()

    @pl.when(jnp.logical_not(has_next))
    def _():
        fut[...] = jnp.zeros_like(fut)

    inv_width = 1.0 / math.sqrt(E)
    valid_lane = jnp.where(lane[0:1, :] + m * FD < length, inv_width, 0.0)
    later = iota((16, FD), 0) + FD
    later_lane = iota((16, FD), 1)
    for k in range(K):
        here = jnp.where(sub == lane + (k + 1), nt(grid[0], predicted[k]), 0.0)
        ahead = jnp.where(later == later_lane + (k + 1), nt(fut[...], predicted[k]), 0.0)
        positive = jnp.sum(here, axis=0, keepdims=True) + jnp.sum(ahead, axis=0, keepdims=True)
        out_ref[0, k, 0:1, :] = positive * valid_lane

    negative = [[jnp.zeros((1, FD), F32) for _ in range(NNEG)] for _ in range(K)]

    def score(dz):
        start = 1 if dz == 0 else 0
        for d in range(start, 4):
            n = dz * 4 + d
            block = rows[n]
            found = [slot_rows + n * SLOT == spot[j] for j in range(NNEG)]
            for k in range(K):
                scores = nt(block, predicted[k])
                for j in range(NNEG):
                    negative[k][j] += jnp.sum(jnp.where(found[j], scores, 0.0), axis=0, keepdims=True)

    for dz in (0, 1, 3, 2):
        sends[dz].wait()
        score(dz)
    up_all.wait_send()
    dn_all.wait_send()
    for k in range(K):
        for j in range(NNEG):
            out_ref[0, k, 1 + j : 2 + j, :] = negative[k][j] * valid_lane


def shards(raw, w_conv, w_query, w_key, w_pred, log_decay, lengths, neg_offset, neg_frame):
    hbm = pl.BlockSpec(memory_space=pl.ANY)
    dma = pltpu.SemaphoreType.DMA
    return pl.pallas_call(
        kernel,
        out_shape=pltpu.VMEM((1, K, 1 + NNEG, FD), F32),
        in_specs=[hbm] * 8 + [pl.BlockSpec(memory_space=pltpu.SMEM)],
        out_specs=pl.BlockSpec(memory_space=pltpu.VMEM),
        scratch_shapes=[
            pltpu.VMEM((FD, FRAME_W), BF16),
            pltpu.VMEM((2 * FRAME_W, E), BF16),
            pltpu.VMEM((E, DA), BF16),
            pltpu.VMEM((E, DA), BF16),
            pltpu.VMEM((K, E, E), BF16),
            pltpu.VMEM((H, FD), F32),
            pltpu.VMEM((NNEG, 1, FD), I32),
            pltpu.VMEM((NNEG, 1, FD), I32),
            pltpu.VMEM((16, FRAME_W), BF16),
            pltpu.VMEM((16, E), BF16),
            pltpu.VMEM((PAD, FD), I32),
            pltpu.VMEM((4, PAD, FD), I32),
            pltpu.VMEM((4, FD, E), BF16),
            pltpu.VMEM((4, 4, SLOT, E), BF16),
            pltpu.VMEM((16, SLOT, E), BF16),
            pltpu.VMEM((4, 4 * PAD, FD), BF16),
            pltpu.VMEM((H, DV + 8, FD), F32),
            pltpu.VMEM((4, DV + 8, FD), F32),
            pltpu.VMEM((4, MSG, FD), BF16),
            pltpu.VMEM((4, MSG, FD), BF16),
            pltpu.VMEM((YMSG, FD), F32),
            pltpu.VMEM((4, YMSG, FD), F32),
            pltpu.VMEM((4, DV, FD), BF16),
            pltpu.VMEM((4, DV, FD), BF16),
            pltpu.VMEM((4, DV, FD), BF16),
            pltpu.VMEM((H, DV, FD), BF16),
            pltpu.VMEM((FD, DA), BF16),
            pltpu.VMEM((H, DV, FD), F32),
            dma((8,)),
            dma((2,)),
            dma((2,)),
            dma((2,)),
            dma((8,)),
            dma((4,)),
            dma((8,)),
            dma((4,)),
            dma((2,)),
            dma((2,)),
            dma((2,)),
        ],
        compiler_params=pltpu.CompilerParams(collective_id=0, has_side_effects=True),
    )(
        raw, w_conv, w_query, w_key, w_pred, log_decay,
        jnp.transpose(neg_offset, (2, 0, 1)), jnp.transpose(neg_frame, (2, 0, 1)), lengths,
    )


def solution(mesh):
    placed = (
        P("batch", "tm", None),
        P(),
        P(),
        P(),
        P(),
        P("batch", None, "tm"),
        P("batch"),
        P("batch", "tm", None),
        P("batch", "tm", None),
    )
    return jax.shard_map(
        shards, mesh=mesh, in_specs=placed, out_specs=P("batch", None, None, "tm"), check_vma=False
    )
```

```python
import functools
import math

import jax
import jax.numpy as jnp
from jax import lax
from jax.experimental import pallas as pl
from jax.experimental.pallas import tpu as pltpu
from jax.sharding import PartitionSpec as P

MESH = pl.DeviceIdType.MESH
F32, BF16, I32 = jnp.float32, jnp.bfloat16, jnp.int32
FD, E, DA, H, FRAME_W, K, NNEG = 128, 512, 1024, 8, 640, 2, 3
DK, DV = DA // H, E // H
SLOT, PAD = 40, 48
CHUNK = FD // 4
BASE = (0, 4, 12, 8)
MSG = DV + 8
YMSG = DV + 8


def nt(a, b):
    return lax.dot_general(a, b, (((1,), (1,)), ((), ())), preferred_element_type=F32)


def nn(a, b):
    return jnp.dot(a, b, preferred_element_type=F32)


def iota(shape, axis):
    return lax.broadcasted_iota(I32, shape, axis)


def kernel(
    raw_hbm, wc_hbm, wq_hbm, wk_hbm, wp_hbm, ld_hbm, off_hbm, frm_hbm, len_ref, out_ref,
    raw, wc, wq, wk, wp, ld, off, frm, halo, fut, want, asked, grid, pick, rows,
    chosen, st_out, st_in, msg_out, msg_in, y_out, y_in, ent_out, ent_in, ent_pair, ent, q_s, inside,
    load_sem, halo_sem, fut_sem, ask_sem, near_sem, far_sem, row_sem, pair_sem, msg_sem, y_sem, ent_sem,
):
    b, m = lax.axis_index("batch"), lax.axis_index("tm")
    zh, x = b // 4, b % 4
    y, zl, c = m // 8, (m // 2) % 4, m % 2

    def remote(src, dst, sems, out, back, dev):
        return pltpu.make_async_remote_copy(
            src_ref=src, dst_ref=dst, send_sem=sems.at[out], recv_sem=sems.at[back],
            device_id=dev, device_id_type=MESH,
        )

    loads = [
        pltpu.make_async_copy(src, dst, load_sem.at[n])
        for n, (src, dst) in enumerate(
            [(raw_hbm.at[0], raw), (wc_hbm, wc), (off_hbm, off), (frm_hbm, frm), (ld_hbm.at[0], ld),
             (wk_hbm, wk), (wq_hbm, wq), (wp_hbm, wp)]
        )
    ]
    loads[0].start()
    loads[1].start()

    z_up, z_dn = (((zh + 1) % 4) * 4 + x, m), (((zh + 3) % 4) * 4 + x, m)
    x_of = [(zh * 4 + (x + d) % 4, m) for d in range(4)]
    pair = (b, m + 1 - 2 * c)
    row_of = [(b, y * 8 + ((zl + d) % 4) * 2 + c) for d in range(4)]
    y_of = [(b, ((y + d) % 4) * 8 + zl * 2 + c) for d in range(4)]
    nxt, prv = (b, jnp.minimum(m + 1, 31)), (b, jnp.maximum(m - 1, 0))
    has_next, has_prev = m < 31, m > 0
    edge_next = jnp.logical_and(c == 1, has_next)
    edge_prev = jnp.logical_and(c == 0, has_prev)

    barrier = pltpu.get_barrier_semaphore()
    for dev in [z_up, z_dn] + x_of[1:] + y_of[1:] + row_of[1:] + [pair]:
        pl.semaphore_signal(barrier, inc=1, device_id=dev, device_id_type=MESH)

    @pl.when(edge_next)
    def _():
        pl.semaphore_signal(barrier, inc=1, device_id=nxt, device_id_type=MESH)

    @pl.when(edge_prev)
    def _():
        pl.semaphore_signal(barrier, inc=1, device_id=prv, device_id_type=MESH)

    for load in loads[2:]:
        load.start()

    for n in range(1, 16):
        rows[n, pl.ds(SLOT, PAD - SLOT), :] = jnp.zeros((PAD - SLOT, E), BF16)

    lane = iota((FD, FD), 1)
    sub = iota((FD, FD), 0)
    length = len_ref[0]
    valid_rows = jnp.where(sub + m * FD < length, 1.0, 0.0)
    valid_rows = jnp.concatenate([valid_rows] * 4, axis=1)

    def encode(hidden, valid):
        u = jax.nn.gelu(hidden)
        return (u * lax.rsqrt(jnp.mean(u * u, axis=-1, keepdims=True) + 1e-05) * valid).astype(BF16)

    loads[0].wait()
    loads[1].wait()
    before = pltpu.roll(nn(raw[...], wc[:FRAME_W, :]), 1, 0)
    now = nn(raw[...], wc[FRAME_W:, :])
    enc = encode(now + before, valid_rows)
    grid[0] = enc

    def part(n):
        return pl.ds(n * CHUNK, CHUNK)

    low, high = pl.ds(0, 2 * CHUNK), pl.ds(2 * CHUNK, 2 * CHUNK)
    up = [remote(grid.at[0, part(n), :], grid.at[1, part(n), :], near_sem, 0, 2 + max(n - 1, 0), z_up) for n in range(4)]
    dn = [remote(grid.at[0, part(n), :], grid.at[3, part(n), :], near_sem, 1, 5 + min(n, 2), z_dn) for n in range(4)]
    up_all, dn_all = remote(grid.at[0], grid.at[1], near_sem, 0, 2, z_up), remote(grid.at[0], grid.at[3], near_sem, 1, 7, z_dn)
    up_rest = remote(grid.at[0, low, :], grid.at[1, low, :], near_sem, 0, 2, z_up)
    dn_rest = remote(grid.at[0, high, :], grid.at[3, high, :], near_sem, 1, 7, z_dn)
    far_up = [remote(grid.at[1, part(n), :], grid.at[2, part(n), :], far_sem, 0, 1, z_up) for n in (3, 2)]
    far_dn = [remote(grid.at[3, part(n), :], grid.at[2, part(n), :], far_sem, 2, 3, z_dn) for n in (1, 0)]
    far_all = [
        remote(grid.at[1, high, :], grid.at[2, high, :], far_sem, 0, 1, z_up),
        remote(grid.at[3, low, :], grid.at[2, low, :], far_sem, 2, 3, z_dn),
    ]
    halo_copy = remote(raw.at[pl.ds(FD - 16, 16), :], halo, halo_sem, 0, 1, nxt)
    fut_copy = remote(grid.at[0, pl.ds(0, 16), :], fut, fut_sem, 0, 1, prv)
    asks = [remote(want, asked.at[d], ask_sem, 0, 1, x_of[(4 - d) % 4]) for d in range(1, 4)]
    asks_all = remote(asked.at[pl.ds(1, 3)], asked.at[pl.ds(1, 3)], ask_sem, 0, 1, x_of[1])

    edges = jnp.where(c == 1, jnp.where(has_next, 1, 0), jnp.where(has_prev, 1, 0))
    pl.semaphore_wait(barrier, 12 + edges)

    @pl.when(has_next)
    def _():
        halo_copy.start()

    up[3].start()
    dn[1].start()

    loads[2].wait()
    loads[3].wait()
    rel_j, frame_j = [], []
    for j in range(NNEG):
        group = (b + off[j] + 1) & 15
        dz = (zh - (group >> 2)) & 3
        rel_j.append(((dz ^ (dz >> 1)) << 2) | ((x - (group & 3)) & 3))
        frame_j.append(frm[j])
    rel_rows = iota((16, FD), 0)
    hit = [jnp.where(rel_rows == rel_j[j], 1, 0) for j in range(NNEG)]
    named = hit[0] + hit[1] + hit[2]
    frame_of = hit[0] * frame_j[0] + hit[1] * frame_j[1] + hit[2] * frame_j[2]
    upto = jnp.where(sub <= lane, 1.0, 0.0).astype(BF16)
    rank = nn(named.astype(F32).astype(BF16), upto).astype(I32) - 1
    spot = [jnp.sum(hit[j] * (rel_rows * PAD + rank), axis=0, keepdims=True) for j in range(NNEG)]
    code = jnp.where(named > 0, rank, -1)
    pad_rows = iota((PAD, FD), 0)
    pad_lane = iota((PAD, FD), 1)
    wanted = jnp.zeros((PAD, FD), I32)
    for r in range(1, 16):
        column = jnp.sum(
            jnp.where(pad_rows == code[r : r + 1, :], frame_of[r : r + 1, :].astype(F32), 0.0), axis=1, keepdims=True
        )
        wanted = jnp.where(pad_lane == r, column.astype(I32), wanted)
    want[...] = wanted
    for copy in asks:
        copy.start()

    loads[4].wait()
    cum = ld[...]
    lane8 = iota((H, FD), 1)
    for shift in (1, 2, 4, 8, 16, 32, 64):
        cum = cum + jnp.where(lane8 >= shift, pltpu.roll(cum, shift, 1), 0.0)
    cum_col = jnp.concatenate([cum, jnp.zeros((FD - H, FD), F32)], axis=0).T
    total = jnp.sum(jnp.where(lane8 == FD - 1, cum, 0.0), axis=1, keepdims=True)
    total_row = jnp.broadcast_to(total, (H, FD))

    @pl.when(has_prev)
    def _():
        halo_copy.wait_recv()

    @pl.when(jnp.logical_not(has_prev))
    def _():
        halo[...] = jnp.zeros_like(halo)

    edge = nn(halo[...], wc[:FRAME_W, :])
    first = iota((16, E), 0) == 0
    top = encode(
        now[:16, :] + jnp.where(first, jnp.broadcast_to(edge[15:16, :], (16, E)), before[:16, :]), valid_rows[:16, :]
    )
    grid[0, pl.ds(0, 16), :] = top
    enc = jnp.concatenate([top, enc[16:, :]], axis=0)
    up[2].start()
    dn[0].start()

    @pl.when(has_prev)
    def _():
        fut_copy.start()

    loads[5].wait()
    enc_t = [enc[:, n * FD : (n + 1) * FD].T for n in range(E // FD)]
    value_t = [enc_t[h // 2][(h % 2) * DV : (h % 2 + 1) * DV, :] for h in range(H)]
    keys = nn(enc, wk[...]).astype(BF16)
    for h in range(H):
        key = keys[:, h * DK : (h + 1) * DK]
        to_end = jnp.exp(total_row[h : h + 1, :] - jnp.broadcast_to(cum_col[:, h : h + 1], (FD, FD)))
        weighted = (key.astype(F32) * to_end).astype(BF16)
        st_out[h, pl.ds(0, DV), :] = nn(value_t[h], weighted)
        st_out[h, pl.ds(DV, 8), :] = jnp.broadcast_to(total_row[h : h + 1, :], (8, FD))
    pair_copy = remote(st_out.at[pl.ds(4 - 4 * c, 4)], st_in, pair_sem, 0, 1, pair)
    pair_copy.start()

    loads[6].wait()
    queries = nn(enc, wq[...]).astype(BF16)
    q_s[...] = queries

    def core_states(n):
        own, other = st_out[4 * c + n], st_in[n]
        return jnp.where(c == 0, own, other), jnp.where(c == 0, other, own)

    pair_copy.wait()
    piece = iota((8, FD), 0)
    for n in range(4):
        early, late = core_states(n)
        joined = jnp.exp(late[DV : DV + 1, :]) * early[:DV, :] + late[:DV, :]
        whole = early[DV : DV + 1, :] + late[DV : DV + 1, :]
        hi = whole.astype(BF16).astype(F32)
        mid = (whole - hi).astype(BF16).astype(F32)
        lo = whole - hi - mid
        pieces = jnp.where(piece == 0, hi, jnp.where(piece == 1, mid, jnp.where(piece == 2, lo, 0.0)))
        msg_out[n, pl.ds(0, DV), :] = joined.astype(BF16)
        msg_out[n, pl.ds(DV, 8), :] = pieces.astype(BF16)
    msgs = [remote(msg_out.at[(zl + d) % 4], msg_in.at[zl], msg_sem, 0, 1, row_of[d]) for d in range(1, 4)]
    msgs_all = remote(msg_out.at[pl.ds(0, 3)], msg_in.at[pl.ds(0, 3)], msg_sem, 0, 1, row_of[1])
    for copy in msgs:
        copy.start()
    msg_in[zl] = msg_out[zl]
    up[1].start()
    dn[3].start()
    up[0].start()
    dn[2].start()

    scale = 1.0 / math.sqrt(DK)
    for h in range(H):
        key = keys[:, h * DK : (h + 1) * DK]
        query = queries[:, h * DK : (h + 1) * DK]
        gap = cum[h : h + 1, :] - jnp.broadcast_to(cum_col[:, h : h + 1], (FD, FD))
        weight = jnp.where(sub <= lane, jnp.exp(jnp.minimum(gap, 0.0)), 0.0)
        probs_t = (nt(key, query) * weight * scale).astype(BF16)
        inside[h] = nn(value_t[h], probs_t)

    asks_all.wait()

    for dz in range(4):
        for d in range(4):
            lists = want[...] if d == 0 else asked[d]
            column = jnp.broadcast_to(lists[:, BASE[dz] + d : BASE[dz] + d + 1], (PAD, FD))
            chosen[dz, pl.ds(d * PAD, PAD), :] = jnp.where(pad_lane == column, 1.0, 0.0).astype(BF16)

    def serve(dz):
        got = nn(chosen[dz], grid[dz]).astype(BF16)
        for d in (2, 1, 3):
            pick[dz, d] = got[d * PAD : d * PAD + SLOT, :]
            remote(pick.at[dz, d], rows.at[BASE[dz] + d, pl.ds(0, SLOT), :], row_sem, dz, 4 + dz, x_of[d]).start()
        if dz > 0:
            rows[BASE[dz], pl.ds(0, SLOT), :] = got[:SLOT, :]
        return remote(pick.at[dz, pl.ds(1, 3)], rows.at[pl.ds(BASE[dz] + 1, 3), pl.ds(0, SLOT), :], row_sem, dz, 4 + dz, x_of[1])

    sends = {0: serve(0)}

    up[3].wait_recv()
    far_up[0].start()
    dn[1].wait_recv()
    far_dn[0].start()

    msgs_all.wait()
    lam = [jnp.sum(msg_in[n, pl.ds(DV, 8), :].astype(F32), axis=0, keepdims=True) for n in range(4)]
    prefix, reach = [jnp.zeros((DV, FD), F32)], [jnp.zeros((1, FD), F32)]
    for n in range(4):
        prefix.append(jnp.exp(lam[n]) * prefix[-1] + msg_in[n, pl.ds(0, DV), :].astype(F32))
        reach.append(reach[-1] + lam[n])
    y_out[pl.ds(0, DV), :] = prefix[4]
    y_out[pl.ds(DV, 8), :] = jnp.broadcast_to(reach[4], (8, FD))
    y_copies = [remote(y_out, y_in.at[(4 - d) % 4], y_sem, 0, 1, y_of[d]) for d in range(1, 4)]
    y_all = remote(y_in.at[pl.ds(1, 3)], y_in.at[pl.ds(1, 3)], y_sem, 0, 1, y_of[1])
    for copy in y_copies:
        copy.start()
    up[2].wait_recv()
    far_up[1].start()
    dn[0].wait_recv()
    far_dn[1].start()

    y_all.wait()
    carry = jnp.zeros((DV, FD), F32)
    for d in range(1, 4):
        step = jnp.exp(y_in[d, pl.ds(DV, 1), :]) * carry + y_in[d, pl.ds(0, DV), :]
        carry = jnp.where(d >= 4 - y, step, carry)
    for n in range(4):
        ent_out[n] = (prefix[n] + jnp.exp(reach[n]) * carry).astype(BF16)
    entries = [remote(ent_out.at[(zl + d) % 4], ent_in.at[zl], ent_sem, 0, 1, row_of[d]) for d in range(1, 4)]
    entries_all = remote(ent_out.at[pl.ds(0, 3)], ent_in.at[pl.ds(0, 3)], ent_sem, 0, 1, row_of[1])
    for copy in entries:
        copy.start()
    ent_in[zl] = ent_out[zl]

    up_rest.wait_recv()
    sends[1] = serve(1)
    dn_rest.wait_recv()
    sends[3] = serve(3)
    for copy in far_all:
        copy.wait()
    sends[2] = serve(2)
    entries_all.wait()
    for n in range(4):
        early, _ = core_states(n)
        at_first = ent_in[n].astype(F32)
        at_second = jnp.exp(early[DV : DV + 1, :]) * at_first + early[:DV, :]
        ent[4 * c + n] = jnp.where(c == 0, at_first, at_second).astype(BF16)
        ent_pair[n] = jnp.where(c == 0, at_second, at_first).astype(BF16)
    back_copy = remote(ent_pair, ent.at[pl.ds(4 * c, 4)], pair_sem, 2, 3, pair)
    back_copy.start()
    @pl.when(has_prev)
    def _():
        fut_copy.wait_send()

    @pl.when(has_next)
    def _():
        fut_copy.wait_recv()
        halo_copy.wait_send()

    @pl.when(jnp.logical_not(has_next))
    def _():
        fut[...] = jnp.zeros_like(fut)

    loads[7].wait()
    back_copy.wait()
    halves = []
    for h in range(H):
        carried = nt(ent[h], q_s[:, h * DK : (h + 1) * DK]) * (jnp.exp(cum[h : h + 1, :]) * scale)
        attended = inside[h] + carried
        halves.append(attended * lax.rsqrt(jnp.mean(attended * attended, axis=0, keepdims=True) + 1e-05))
    context = jnp.concatenate(
        [jnp.concatenate(halves[2 * n : 2 * n + 2], axis=0).T.astype(BF16) for n in range(E // FD)], axis=1
    )
    predicted = [nn(context, wp[k]).astype(BF16) for k in range(K)]

    for dz in (0, 1, 3):
        sends[dz].wait()
    predicted = jnp.concatenate(predicted, axis=0)
    inv_width = 1.0 / math.sqrt(E)
    valid_lane = jnp.where(lane[0:1, :] + m * FD < length, inv_width, 0.0)
    later = iota((16, FD), 0) + FD
    later_lane = iota((16, FD), 1)
    here, ahead = nt(grid[0], predicted), nt(fut[...], predicted)
    for k in range(K):
        span = slice(k * FD, (k + 1) * FD)
        positive = jnp.sum(jnp.where(sub == lane + (k + 1), here[:, span], 0.0), axis=0, keepdims=True) + jnp.sum(
            jnp.where(later == later_lane + (k + 1), ahead[:, span], 0.0), axis=0, keepdims=True
        )
        out_ref[0, k, 0:1, :] = positive * valid_lane

    negative = [[jnp.zeros((1, FD), F32) for _ in range(NNEG)] for _ in range(K)]

    def score(start, stop):
        count = (stop - start) * PAD
        scores = nt(rows[pl.ds(start, stop - start)].reshape(count, E), predicted)
        place = iota((count, FD), 0) + start * PAD
        for j in range(NNEG):
            found = place == spot[j]
            for k in range(K):
                negative[k][j] += jnp.sum(
                    jnp.where(found, scores[:, k * FD : (k + 1) * FD], 0.0), axis=0, keepdims=True
                )

    score(1, 12)
    sends[2].wait()
    score(12, 16)
    for k in range(K):
        for j in range(NNEG):
            out_ref[0, k, 1 + j : 2 + j, :] = negative[k][j] * valid_lane
    up_all.wait_send()
    dn_all.wait_send()


def shards(raw, w_conv, w_query, w_key, w_pred, log_decay, lengths, neg_offset, neg_frame):
    hbm = pl.BlockSpec(memory_space=pl.ANY)
    dma = pltpu.SemaphoreType.DMA
    return pl.pallas_call(
        kernel,
        out_shape=pltpu.VMEM((1, K, 1 + NNEG, FD), F32),
        in_specs=[hbm] * 8 + [pl.BlockSpec(memory_space=pltpu.SMEM)],
        out_specs=pl.BlockSpec(memory_space=pltpu.VMEM),
        scratch_shapes=[
            pltpu.VMEM((FD, FRAME_W), BF16),
            pltpu.VMEM((2 * FRAME_W, E), BF16),
            pltpu.VMEM((E, DA), BF16),
            pltpu.VMEM((E, DA), BF16),
            pltpu.VMEM((K, E, E), BF16),
            pltpu.VMEM((H, FD), F32),
            pltpu.VMEM((NNEG, 1, FD), I32),
            pltpu.VMEM((NNEG, 1, FD), I32),
            pltpu.VMEM((16, FRAME_W), BF16),
            pltpu.VMEM((16, E), BF16),
            pltpu.VMEM((PAD, FD), I32),
            pltpu.VMEM((4, PAD, FD), I32),
            pltpu.VMEM((4, FD, E), BF16),
            pltpu.VMEM((4, 4, SLOT, E), BF16),
            pltpu.VMEM((16, PAD, E), BF16),
            pltpu.VMEM((4, 4 * PAD, FD), BF16),
            pltpu.VMEM((H, DV + 8, FD), F32),
            pltpu.VMEM((4, DV + 8, FD), F32),
            pltpu.VMEM((4, MSG, FD), BF16),
            pltpu.VMEM((4, MSG, FD), BF16),
            pltpu.VMEM((YMSG, FD), F32),
            pltpu.VMEM((4, YMSG, FD), F32),
            pltpu.VMEM((4, DV, FD), BF16),
            pltpu.VMEM((4, DV, FD), BF16),
            pltpu.VMEM((4, DV, FD), BF16),
            pltpu.VMEM((H, DV, FD), BF16),
            pltpu.VMEM((FD, DA), BF16),
            pltpu.VMEM((H, DV, FD), F32),
            dma((8,)),
            dma((2,)),
            dma((2,)),
            dma((2,)),
            dma((8,)),
            dma((4,)),
            dma((8,)),
            dma((4,)),
            dma((2,)),
            dma((2,)),
            dma((2,)),
        ],
        compiler_params=pltpu.CompilerParams(collective_id=0, has_side_effects=True),
    )(
        raw, w_conv, w_query, w_key, w_pred, log_decay,
        jnp.transpose(neg_offset, (2, 0, 1)), jnp.transpose(neg_frame, (2, 0, 1)), lengths,
    )


def solution(mesh):
    placed = (
        P("batch", "tm", None),
        P(),
        P(),
        P(),
        P(),
        P("batch", None, "tm"),
        P("batch"),
        P("batch", "tm", None),
        P("batch", "tm", None),
    )
    return jax.shard_map(
        shards, mesh=mesh, in_specs=placed, out_specs=P("batch", None, None, "tm"), check_vma=False
    )
```

```python
import functools
import math

import jax
import jax.numpy as jnp
from jax import lax
from jax.experimental import pallas as pl
from jax.experimental.pallas import tpu as pltpu
from jax.sharding import PartitionSpec as P

MESH = pl.DeviceIdType.MESH
F32, BF16, I32 = jnp.float32, jnp.bfloat16, jnp.int32
FD, E, DA, H, FRAME_W, K, NNEG = 128, 512, 1024, 8, 640, 2, 3
DK, DV = DA // H, E // H
SLOT, PAD = 40, 48
CHUNK = FD // 4
BASE = (0, 4, 12, 8)
MSG = DV + 8
YMSG = DV + 8


def nt(a, b):
    return lax.dot_general(a, b, (((1,), (1,)), ((), ())), preferred_element_type=F32)


def nn(a, b):
    return jnp.dot(a, b, preferred_element_type=F32)


def iota(shape, axis):
    return lax.broadcasted_iota(I32, shape, axis)


def kernel(
    raw_hbm, wc_hbm, wq_hbm, wk_hbm, wp_hbm, ld_hbm, off_hbm, frm_hbm, len_ref, out_ref,
    raw, wc, wq, wk, wp, ld, off, frm, halo, fut, want, asked, grid, pick, rows,
    chosen, st_out, st_in, msg_out, msg_in, y_out, y_in, ent_out, ent_in, ent_pair, ent, q_s, inside,
    load_sem, halo_sem, fut_sem, ask_sem, near_sem, far_sem, row_sem, pair_sem, msg_sem, y_sem, ent_sem,
):
    b, m = lax.axis_index("batch"), lax.axis_index("tm")
    zh, x = b // 4, b % 4
    y, zl, c = m // 8, (m // 2) % 4, m % 2

    def remote(src, dst, sems, out, back, dev):
        return pltpu.make_async_remote_copy(
            src_ref=src, dst_ref=dst, send_sem=sems.at[out], recv_sem=sems.at[back],
            device_id=dev, device_id_type=MESH,
        )

    loads = [
        pltpu.make_async_copy(src, dst, load_sem.at[n])
        for n, (src, dst) in enumerate(
            [(raw_hbm.at[0], raw), (wc_hbm, wc), (off_hbm, off), (frm_hbm, frm), (ld_hbm.at[0], ld),
             (wk_hbm, wk), (wq_hbm, wq), (wp_hbm, wp)]
        )
    ]
    loads[0].start()
    loads[1].start()

    z_up, z_dn = (((zh + 1) % 4) * 4 + x, m), (((zh + 3) % 4) * 4 + x, m)
    x_of = [(zh * 4 + (x + d) % 4, m) for d in range(4)]
    pair = (b, m + 1 - 2 * c)
    row_of = [(b, y * 8 + ((zl + d) % 4) * 2 + c) for d in range(4)]
    y_of = [(b, ((y + d) % 4) * 8 + zl * 2 + c) for d in range(4)]
    nxt, prv = (b, jnp.minimum(m + 1, 31)), (b, jnp.maximum(m - 1, 0))
    has_next, has_prev = m < 31, m > 0
    edge_next = jnp.logical_and(c == 1, has_next)
    edge_prev = jnp.logical_and(c == 0, has_prev)

    barrier = pltpu.get_barrier_semaphore()
    for dev in [z_up, z_dn] + x_of[1:] + y_of[1:] + row_of[1:] + [pair]:
        pl.semaphore_signal(barrier, inc=1, device_id=dev, device_id_type=MESH)

    @pl.when(edge_next)
    def _():
        pl.semaphore_signal(barrier, inc=1, device_id=nxt, device_id_type=MESH)

    @pl.when(edge_prev)
    def _():
        pl.semaphore_signal(barrier, inc=1, device_id=prv, device_id_type=MESH)

    for load in loads[2:]:
        load.start()

    for n in range(1, 16):
        rows[n, pl.ds(SLOT, PAD - SLOT), :] = jnp.zeros((PAD - SLOT, E), BF16)

    lane = iota((FD, FD), 1)
    sub = iota((FD, FD), 0)
    length = len_ref[0]
    valid_rows = jnp.where(sub + m * FD < length, 1.0, 0.0)
    valid_rows = jnp.concatenate([valid_rows] * 4, axis=1)

    def encode(hidden, valid):
        u = jax.nn.gelu(hidden)
        return (u * lax.rsqrt(jnp.mean(u * u, axis=-1, keepdims=True) + 1e-05) * valid).astype(BF16)

    loads[0].wait()
    loads[1].wait()
    before = pltpu.roll(nn(raw[...], wc[:FRAME_W, :]), 1, 0)
    now = nn(raw[...], wc[FRAME_W:, :])
    enc = encode(now + before, valid_rows)
    grid[0] = enc

    def part(n):
        return pl.ds(n * CHUNK, CHUNK)

    low, high = pl.ds(0, 2 * CHUNK), pl.ds(2 * CHUNK, 2 * CHUNK)
    up = [remote(grid.at[0, part(n), :], grid.at[1, part(n), :], near_sem, 0, 2 + max(n - 1, 0), z_up) for n in range(4)]
    dn = [remote(grid.at[0, part(n), :], grid.at[3, part(n), :], near_sem, 1, 5 + min(n, 2), z_dn) for n in range(4)]
    up_all, dn_all = remote(grid.at[0], grid.at[1], near_sem, 0, 2, z_up), remote(grid.at[0], grid.at[3], near_sem, 1, 7, z_dn)
    near_1 = jnp.where(zl < 2, 3, 1)
    near_3 = 4 - near_1

    def rest(dz):
        half = pl.ds(pl.multiple_of((dz // 2) * 2 * CHUNK, 2 * CHUNK), 2 * CHUNK)
        return remote(grid.at[0, half, :], grid.at[dz, half, :], near_sem, dz // 2, 2 + (dz // 2) * 5, z_up)

    far_up = [remote(grid.at[1, part(n), :], grid.at[2, part(n), :], far_sem, 0, 1, z_up) for n in (3, 2)]
    far_dn = [remote(grid.at[3, part(n), :], grid.at[2, part(n), :], far_sem, 2, 3, z_dn) for n in (1, 0)]
    far_all = [
        remote(grid.at[1, high, :], grid.at[2, high, :], far_sem, 0, 1, z_up),
        remote(grid.at[3, low, :], grid.at[2, low, :], far_sem, 2, 3, z_dn),
    ]
    halo_copy = remote(raw.at[pl.ds(FD - 16, 16), :], halo, halo_sem, 0, 1, nxt)
    fut_copy = remote(grid.at[0, pl.ds(0, 16), :], fut, fut_sem, 0, 1, prv)
    asks = [remote(want, asked.at[d], ask_sem, 0, 1, x_of[(4 - d) % 4]) for d in range(1, 4)]
    asks_all = remote(asked.at[pl.ds(1, 3)], asked.at[pl.ds(1, 3)], ask_sem, 0, 1, x_of[1])

    edges = jnp.where(c == 1, jnp.where(has_next, 1, 0), jnp.where(has_prev, 1, 0))
    pl.semaphore_wait(barrier, 12 + edges)

    @pl.when(has_next)
    def _():
        halo_copy.start()

    up[3].start()
    dn[1].start()

    loads[2].wait()
    loads[3].wait()
    rel_j, frame_j = [], []
    for j in range(NNEG):
        group = (b + off[j] + 1) & 15
        dz = (zh - (group >> 2)) & 3
        rel_j.append(((dz ^ (dz >> 1)) << 2) | ((x - (group & 3)) & 3))
        frame_j.append(frm[j])
    rel_rows = iota((16, FD), 0)
    hit = [jnp.where(rel_rows == rel_j[j], 1, 0) for j in range(NNEG)]
    named = hit[0] + hit[1] + hit[2]
    frame_of = hit[0] * frame_j[0] + hit[1] * frame_j[1] + hit[2] * frame_j[2]
    upto = jnp.where(sub <= lane, 1.0, 0.0).astype(BF16)
    rank = nn(named.astype(F32).astype(BF16), upto).astype(I32) - 1
    spot = [jnp.sum(hit[j] * (rel_rows * PAD + rank), axis=0, keepdims=True) for j in range(NNEG)]
    code = jnp.where(named > 0, rank, -1)
    pad_rows = iota((PAD, FD), 0)
    pad_lane = iota((PAD, FD), 1)
    wanted = jnp.zeros((PAD, FD), I32)
    for r in range(1, 16):
        column = jnp.sum(
            jnp.where(pad_rows == code[r : r + 1, :], frame_of[r : r + 1, :].astype(F32), 0.0), axis=1, keepdims=True
        )
        wanted = jnp.where(pad_lane == r, column.astype(I32), wanted)
    want[...] = wanted
    for copy in asks:
        copy.start()

    loads[4].wait()
    cum = ld[...]
    lane8 = iota((H, FD), 1)
    for shift in (1, 2, 4, 8, 16, 32, 64):
        cum = cum + jnp.where(lane8 >= shift, pltpu.roll(cum, shift, 1), 0.0)
    cum_col = jnp.concatenate([cum, jnp.zeros((FD - H, FD), F32)], axis=0).T
    total = jnp.sum(jnp.where(lane8 == FD - 1, cum, 0.0), axis=1, keepdims=True)
    total_row = jnp.broadcast_to(total, (H, FD))

    @pl.when(has_prev)
    def _():
        halo_copy.wait_recv()

    @pl.when(jnp.logical_not(has_prev))
    def _():
        halo[...] = jnp.zeros_like(halo)

    edge = nn(halo[...], wc[:FRAME_W, :])
    first = iota((16, E), 0) == 0
    top = encode(
        now[:16, :] + jnp.where(first, jnp.broadcast_to(edge[15:16, :], (16, E)), before[:16, :]), valid_rows[:16, :]
    )
    grid[0, pl.ds(0, 16), :] = top
    enc = jnp.concatenate([top, enc[16:, :]], axis=0)
    up[2].start()
    dn[0].start()

    @pl.when(has_prev)
    def _():
        fut_copy.start()

    loads[5].wait()
    enc_t = [enc[:, n * FD : (n + 1) * FD].T for n in range(E // FD)]
    value_t = [enc_t[h // 2][(h % 2) * DV : (h % 2 + 1) * DV, :] for h in range(H)]
    keys = nn(enc, wk[...]).astype(BF16)
    for h in range(H):
        key = keys[:, h * DK : (h + 1) * DK]
        to_end = jnp.exp(total_row[h : h + 1, :] - jnp.broadcast_to(cum_col[:, h : h + 1], (FD, FD)))
        weighted = (key.astype(F32) * to_end).astype(BF16)
        st_out[h, pl.ds(0, DV), :] = nn(value_t[h], weighted)
        st_out[h, pl.ds(DV, 8), :] = jnp.broadcast_to(total_row[h : h + 1, :], (8, FD))
    pair_copy = remote(st_out.at[pl.ds(4 - 4 * c, 4)], st_in, pair_sem, 0, 1, pair)
    pair_copy.start()

    loads[6].wait()
    queries = nn(enc, wq[...]).astype(BF16)
    q_s[...] = queries

    def core_states(n):
        own, other = st_out[4 * c + n], st_in[n]
        return jnp.where(c == 0, own, other), jnp.where(c == 0, other, own)

    pair_copy.wait()
    piece = iota((8, FD), 0)
    for n in range(4):
        early, late = core_states(n)
        joined = jnp.exp(late[DV : DV + 1, :]) * early[:DV, :] + late[:DV, :]
        whole = early[DV : DV + 1, :] + late[DV : DV + 1, :]
        hi = whole.astype(BF16).astype(F32)
        mid = (whole - hi).astype(BF16).astype(F32)
        lo = whole - hi - mid
        pieces = jnp.where(piece == 0, hi, jnp.where(piece == 1, mid, jnp.where(piece == 2, lo, 0.0)))
        msg_out[n, pl.ds(0, DV), :] = joined.astype(BF16)
        msg_out[n, pl.ds(DV, 8), :] = pieces.astype(BF16)
    msgs = [remote(msg_out.at[(zl + d) % 4], msg_in.at[zl], msg_sem, 0, 1, row_of[d]) for d in range(1, 4)]
    msgs_all = remote(msg_out.at[pl.ds(0, 3)], msg_in.at[pl.ds(0, 3)], msg_sem, 0, 1, row_of[1])
    for copy in msgs:
        copy.start()
    msg_in[zl] = msg_out[zl]
    up[1].start()
    dn[3].start()

    scale = 1.0 / math.sqrt(DK)
    for h in range(H):
        key = keys[:, h * DK : (h + 1) * DK]
        query = queries[:, h * DK : (h + 1) * DK]
        gap = cum[h : h + 1, :] - jnp.broadcast_to(cum_col[:, h : h + 1], (FD, FD))
        weight = jnp.where(sub <= lane, jnp.exp(jnp.minimum(gap, 0.0)), 0.0)
        probs_t = (nt(key, query) * weight * scale).astype(BF16)
        inside[h] = nn(value_t[h], probs_t)

    up[0].start()
    dn[2].start()

    asks_all.wait()

    for dz in range(4):
        for d in range(4):
            lists = want[...] if d == 0 else asked[d]
            column = jnp.broadcast_to(lists[:, BASE[dz] + d : BASE[dz] + d + 1], (PAD, FD))
            chosen[dz, pl.ds(d * PAD, PAD), :] = jnp.where(pad_lane == column, 1.0, 0.0).astype(BF16)

    def serve(dz, base):
        got = nn(chosen[dz], grid[dz]).astype(BF16)
        for d in (2, 1, 3):
            pick[dz, d] = got[d * PAD : d * PAD + SLOT, :]
            remote(pick.at[dz, d], rows.at[base + d, pl.ds(0, SLOT), :], row_sem, dz, 4 + dz, x_of[d]).start()
        if base is not BASE[0]:
            rows[base, pl.ds(0, SLOT), :] = got[:SLOT, :]
        return remote(
            pick.at[dz, pl.ds(1, 3)], rows.at[pl.ds(base + 1, 3), pl.ds(0, SLOT), :], row_sem, dz, 4 + dz, x_of[1]
        )

    sends = {0: serve(0, BASE[0])}

    up[3].wait_recv()
    far_up[0].start()
    dn[1].wait_recv()
    far_dn[0].start()

    msgs_all.wait()
    lam = [jnp.sum(msg_in[n, pl.ds(DV, 8), :].astype(F32), axis=0, keepdims=True) for n in range(4)]
    prefix, reach = [jnp.zeros((DV, FD), F32)], [jnp.zeros((1, FD), F32)]
    for n in range(4):
        prefix.append(jnp.exp(lam[n]) * prefix[-1] + msg_in[n, pl.ds(0, DV), :].astype(F32))
        reach.append(reach[-1] + lam[n])
    y_out[pl.ds(0, DV), :] = prefix[4]
    y_out[pl.ds(DV, 8), :] = jnp.broadcast_to(reach[4], (8, FD))
    y_copies = [remote(y_out, y_in.at[(4 - d) % 4], y_sem, 0, 1, y_of[d]) for d in range(1, 4)]
    y_all = remote(y_in.at[pl.ds(1, 3)], y_in.at[pl.ds(1, 3)], y_sem, 0, 1, y_of[1])
    for copy in y_copies:
        copy.start()
    up[2].wait_recv()
    far_up[1].start()
    dn[0].wait_recv()
    far_dn[1].start()

    y_all.wait()
    carry = jnp.zeros((DV, FD), F32)
    for d in range(1, 4):
        step = jnp.exp(y_in[d, pl.ds(DV, 1), :]) * carry + y_in[d, pl.ds(0, DV), :]
        carry = jnp.where(d >= 4 - y, step, carry)
    for n in range(4):
        ent_out[n] = (prefix[n] + jnp.exp(reach[n]) * carry).astype(BF16)
    entries = [remote(ent_out.at[(zl + d) % 4], ent_in.at[zl], ent_sem, 0, 1, row_of[d]) for d in range(1, 4)]
    entries_all = remote(ent_out.at[pl.ds(0, 3)], ent_in.at[pl.ds(0, 3)], ent_sem, 0, 1, row_of[1])
    for copy in entries:
        copy.start()
    ent_in[zl] = ent_out[zl]

    rest(near_1).wait_recv()
    sends[1] = serve(near_1, 2 * near_1 + 2)
    rest(near_3).wait_recv()
    sends[3] = serve(near_3, 2 * near_3 + 2)
    for copy in far_all:
        copy.wait()
    sends[2] = serve(2, BASE[2])
    entries_all.wait()
    for n in range(4):
        early, _ = core_states(n)
        at_first = ent_in[n].astype(F32)
        at_second = jnp.exp(early[DV : DV + 1, :]) * at_first + early[:DV, :]
        ent[4 * c + n] = jnp.where(c == 0, at_first, at_second).astype(BF16)
        ent_pair[n] = jnp.where(c == 0, at_second, at_first).astype(BF16)
    back_copy = remote(ent_pair, ent.at[pl.ds(4 * c, 4)], pair_sem, 2, 3, pair)
    back_copy.start()
    @pl.when(has_prev)
    def _():
        fut_copy.wait_send()

    @pl.when(has_next)
    def _():
        fut_copy.wait_recv()
        halo_copy.wait_send()

    @pl.when(jnp.logical_not(has_next))
    def _():
        fut[...] = jnp.zeros_like(fut)

    loads[7].wait()
    back_copy.wait()
    halves = []
    for h in range(H):
        carried = nt(ent[h], q_s[:, h * DK : (h + 1) * DK]) * (jnp.exp(cum[h : h + 1, :]) * scale)
        attended = inside[h] + carried
        halves.append(attended * lax.rsqrt(jnp.mean(attended * attended, axis=0, keepdims=True) + 1e-05))
    context = jnp.concatenate(
        [jnp.concatenate(halves[2 * n : 2 * n + 2], axis=0).T.astype(BF16) for n in range(E // FD)], axis=1
    )
    predicted = [nn(context, wp[k]).astype(BF16) for k in range(K)]

    for dz in (0, 1, 3):
        sends[dz].wait()
    predicted = jnp.concatenate(predicted, axis=0)
    inv_width = 1.0 / math.sqrt(E)
    valid_lane = jnp.where(lane[0:1, :] + m * FD < length, inv_width, 0.0)
    later = iota((16, FD), 0) + FD
    later_lane = iota((16, FD), 1)
    here, ahead = nt(grid[0], predicted), nt(fut[...], predicted)
    for k in range(K):
        span = slice(k * FD, (k + 1) * FD)
        positive = jnp.sum(jnp.where(sub == lane + (k + 1), here[:, span], 0.0), axis=0, keepdims=True) + jnp.sum(
            jnp.where(later == later_lane + (k + 1), ahead[:, span], 0.0), axis=0, keepdims=True
        )
        out_ref[0, k, 0:1, :] = positive * valid_lane

    negative = [[jnp.zeros((1, FD), F32) for _ in range(NNEG)] for _ in range(K)]

    def score(start, stop):
        count = (stop - start) * PAD
        scores = nt(rows[pl.ds(start, stop - start)].reshape(count, E), predicted)
        place = iota((count, FD), 0) + start * PAD
        for j in range(NNEG):
            found = place == spot[j]
            for k in range(K):
                negative[k][j] += jnp.sum(
                    jnp.where(found, scores[:, k * FD : (k + 1) * FD], 0.0), axis=0, keepdims=True
                )

    score(1, 12)
    sends[2].wait()
    score(12, 16)
    for k in range(K):
        for j in range(NNEG):
            out_ref[0, k, 1 + j : 2 + j, :] = negative[k][j] * valid_lane
    up_all.wait_send()
    dn_all.wait_send()


def shards(raw, w_conv, w_query, w_key, w_pred, log_decay, lengths, neg_offset, neg_frame):
    hbm = pl.BlockSpec(memory_space=pl.ANY)
    dma = pltpu.SemaphoreType.DMA
    return pl.pallas_call(
        kernel,
        out_shape=pltpu.VMEM((1, K, 1 + NNEG, FD), F32),
        in_specs=[hbm] * 8 + [pl.BlockSpec(memory_space=pltpu.SMEM)],
        out_specs=pl.BlockSpec(memory_space=pltpu.VMEM),
        scratch_shapes=[
            pltpu.VMEM((FD, FRAME_W), BF16),
            pltpu.VMEM((2 * FRAME_W, E), BF16),
            pltpu.VMEM((E, DA), BF16),
            pltpu.VMEM((E, DA), BF16),
            pltpu.VMEM((K, E, E), BF16),
            pltpu.VMEM((H, FD), F32),
            pltpu.VMEM((NNEG, 1, FD), I32),
            pltpu.VMEM((NNEG, 1, FD), I32),
            pltpu.VMEM((16, FRAME_W), BF16),
            pltpu.VMEM((16, E), BF16),
            pltpu.VMEM((PAD, FD), I32),
            pltpu.VMEM((4, PAD, FD), I32),
            pltpu.VMEM((4, FD, E), BF16),
            pltpu.VMEM((4, 4, SLOT, E), BF16),
            pltpu.VMEM((16, PAD, E), BF16),
            pltpu.VMEM((4, 4 * PAD, FD), BF16),
            pltpu.VMEM((H, DV + 8, FD), F32),
            pltpu.VMEM((4, DV + 8, FD), F32),
            pltpu.VMEM((4, MSG, FD), BF16),
            pltpu.VMEM((4, MSG, FD), BF16),
            pltpu.VMEM((YMSG, FD), F32),
            pltpu.VMEM((4, YMSG, FD), F32),
            pltpu.VMEM((4, DV, FD), BF16),
            pltpu.VMEM((4, DV, FD), BF16),
            pltpu.VMEM((4, DV, FD), BF16),
            pltpu.VMEM((H, DV, FD), BF16),
            pltpu.VMEM((FD, DA), BF16),
            pltpu.VMEM((H, DV, FD), F32),
            dma((8,)),
            dma((2,)),
            dma((2,)),
            dma((2,)),
            dma((8,)),
            dma((4,)),
            dma((8,)),
            dma((4,)),
            dma((2,)),
            dma((2,)),
            dma((2,)),
        ],
        compiler_params=pltpu.CompilerParams(collective_id=0, has_side_effects=True),
    )(
        raw, w_conv, w_query, w_key, w_pred, log_decay,
        jnp.transpose(neg_offset, (2, 0, 1)), jnp.transpose(neg_frame, (2, 0, 1)), lengths,
    )


def solution(mesh):
    placed = (
        P("batch", "tm", None),
        P(),
        P(),
        P(),
        P(),
        P("batch", None, "tm"),
        P("batch"),
        P("batch", "tm", None),
        P("batch", "tm", None),
    )
    return jax.shard_map(
        shards, mesh=mesh, in_specs=placed, out_specs=P("batch", None, None, "tm"), check_vma=False
    )
```
